32 devices in a mesh: grp: 2 (over y), row: 4 (over z), col: 2 (over x), sub: 2 (over core).
Axes of the slice: x: 2, y: 2, z: 4, core: 2. Of those that a mesh axis runs over, the one named last changes fastest.
Arguments:
- pair: bfloat16 [768, 384, 128], P(('grp', 'row'), ('col', 'sub')), parts along dimension 0, may hold values from -6 to 6
- chain_ids: int32 [768], P('grp'), parts along dimension 0, may hold values from 0 to 3, never falling along the last dimension, each value on 1 to 192 neighbouring positions
- residue_mask: int32 [768], P('grp'), parts along dimension 0, may hold values from 0 to 1, as said below
- chain_vec: float32 [128], replicated, may hold values from -4 to 4
- tri_in: bfloat16 [128, 512], replicated, may hold values from -0.5 to 0.5
- tri_gate: bfloat16 [128, 128], replicated, may hold values from -0.5 to 0.5
- tri_out: bfloat16 [128, 128], replicated, may hold values from -0.5 to 0.5
- att_query: bfloat16 [128, 256], replicated, may hold values from -0.5 to 0.5
- att_kv: bfloat16 [128, 256], replicated, may hold values from -0.5 to 0.5
- att_bias: bfloat16 [128, 4], replicated, may hold values from -0.5 to 0.5
- att_out: bfloat16 [128, 128], replicated, may hold values from -0.5 to 0.5
Outputs:
- updated: bfloat16 [768, 384, 128], P(('grp', 'row'), ('col', 'sub')), parts along dimension 0
The draws below stay inside these ranges and needn't reach their ends.
There are 2 independent parts, one for each index of `grp`. The reference program is written for one: setup_inputs(seed, part) draws one part's arguments, and reference() takes and returns one part's arrays. A program takes and returns all parts, laid end to end along the dimension named above; an argument that names none is the same for every part. Nothing has to cross between parts.
Inputs may be any that keep to these rules, and one draw needn't show every extreme that they name: `chain_ids`: chains are runs of consecutive residues. `residue_mask`: 1 on residues 0 to L - 1 and 0 after them, with L between 192 and 384.
All inputs are finite; a program needn't handle non-finite values.
Results may differ from the reference program's by a relative error of at most 0.009.
Values may be sent and summed in bfloat16 or wider, within the bound.
A program may use at most 128 MiB of HBM per device.

```python
import math
import jax
import jax.numpy as jnp
import numpy as np
from jax import lax

CHANNELS = 128
HEADS = 4
HEAD_DIM = 32
RESIDUES = 384


def draw_residue_mask(key, part):
    limit = jax.random.randint(jax.random.fold_in(key, 11), (), RESIDUES // 2, RESIDUES + 1)
    return (jnp.arange(RESIDUES) < limit).astype(jnp.int32)


def level_of(stream_key, dims, split, smallest, high):
    gain = 1.0
    for axis_at, blocks in split:
        heights = jax.random.uniform(jax.random.fold_in(jax.random.fold_in(stream_key, 6), axis_at), (blocks,), jnp.float32, smallest / len(split), high / len(split))
        gain = gain * jnp.repeat(jnp.exp(heights), dims[axis_at] // blocks).reshape((-1,) + (1,) * (len(dims) - 1 - axis_at))
    return gain


def length_profile(amount, total, bound, lean):
    portions = [(1 << 20) // math.isqrt(rank ** lean) + 1 for rank in range(2, amount + 1)]
    rest, holding = total - bound - (amount - 1), [1] * (amount - 1)
    while rest > 0:
        movable = [i for i in range(amount - 1) if holding[i] < bound]
        whole, remaining = sum([portions[i] for i in movable]), rest
        for i in movable:
            addition = min(bound - holding[i], max(1, remaining * portions[i] // whole), rest)
            holding[i] = holding[i] + addition
            rest = rest - addition
    return np.array([bound] + holding)


def ragged(stream_key, amount, total, reach, lean):
    if amount == 2:
        one = jax.random.randint(stream_key, (), max(1, total - reach), min(reach, total - 1) + 1)
        return jnp.stack([one, total - one])
    lengths = jnp.asarray(length_profile(amount, total, reach, lean), jnp.int32)
    pairs = (amount - 1) // 2
    source_of, taker = lengths[1:1 + 2 * pairs:2], lengths[2:2 + 2 * pairs:2]
    room = jnp.minimum(source_of - 1, reach - taker)
    moved = jax.random.randint(jax.random.fold_in(stream_key, 1), (pairs,), 0, 1 << 20) % (room + 1)
    lengths = lengths.at[1:1 + 2 * pairs:2].set(source_of - moved).at[2:2 + 2 * pairs:2].set(taker + moved)
    return lengths[jax.random.permutation(jax.random.fold_in(stream_key, 2), amount)]


def noise(key, shape, width, most, cuts=(), dtype=jnp.bfloat16):
    factor_of = level_of(key, shape, cuts, -0.22, 0.18) if cuts else 1.0
    entries = jax.random.normal(key, shape, jnp.float32) * width * factor_of
    return jnp.minimum(jnp.maximum(entries, -most), most).astype(dtype)


def setup_inputs(seed: int = 0, part: int = 0) -> dict:
    key_list = jax.random.split(jax.random.key(seed), 12)
    part_splits = jax.random.split(jax.random.fold_in(key_list[11], part), 12)
    pair = noise(part_splits[0], (RESIDUES, RESIDUES, CHANNELS), 1.0, 6.0, ((0, 4), (1, 4)))
    chain_ids = jnp.searchsorted(jnp.cumsum(ragged(part_splits[1], 4, RESIDUES, RESIDUES // 2, 0)), jnp.arange(RESIDUES), side="right").astype(jnp.int32)
    residue_mask = draw_residue_mask(jax.random.fold_in(jax.random.fold_in(key_list[11], part), 71), part)
    chain_vec = noise(key_list[3], (CHANNELS,), 1.0, 4.0, (), jnp.float32)
    tri_in = noise(key_list[4], (CHANNELS, 4 * CHANNELS), CHANNELS ** -0.5, 0.5)
    tri_gate = noise(key_list[5], (CHANNELS, CHANNELS), CHANNELS ** -0.5, 0.5)
    tri_out = noise(key_list[6], (CHANNELS, CHANNELS), CHANNELS ** -0.5, 0.5)
    att_query = noise(key_list[7], (CHANNELS, 2 * HEADS * HEAD_DIM), CHANNELS ** -0.5, 0.5)
    att_kv = noise(key_list[8], (CHANNELS, 2 * HEADS * HEAD_DIM), CHANNELS ** -0.5, 0.5)
    att_bias = noise(key_list[9], (CHANNELS, HEADS), CHANNELS ** -0.5, 0.5)
    att_out = noise(key_list[10], (HEADS * HEAD_DIM, CHANNELS), (HEADS * HEAD_DIM) ** -0.5, 0.5)
    return {"pair": pair, "chain_ids": chain_ids, "residue_mask": residue_mask, "chain_vec": chain_vec, "tri_in": tri_in, "tri_gate": tri_gate, "tri_out": tri_out, "att_query": att_query, "att_kv": att_kv, "att_bias": att_bias, "att_out": att_out}


EPSILON = 1e-05

def layer_norm(values):
    average = lax.optimization_barrier(jnp.mean(values, axis=-1, keepdims=True))
    centred = values - average
    spread = lax.optimization_barrier(jnp.mean(centred * centred, axis=-1, keepdims=True))
    return centred * lax.rsqrt(spread + EPSILON)

def reference(pair, chain_ids, residue_mask, chain_vec, tri_in, tri_gate, tri_out, att_query, att_kv, att_bias, att_out):
    length = pair.shape[0]
    channels = pair.shape[2]
    heads_width = HEADS * HEAD_DIM
    living = residue_mask.astype(jnp.float32)
    pair_mask = living[:, None] * living[None, :]
    same_chain = (chain_ids[:, None] == chain_ids[None, :]).astype(jnp.float32)
    start_pair = pair.astype(jnp.float32) + same_chain[:, :, None] * chain_vec
    normed = layer_norm(start_pair).astype(jnp.bfloat16)
    flat_rows = normed.reshape(length * length, channels)
    projected = jnp.dot(flat_rows, tri_in, preferred_element_type=jnp.float32).reshape(length, length, 4 * channels)
    left_side = (jax.nn.sigmoid(projected[..., channels:2 * channels]) * projected[..., :channels] * pair_mask[..., None]).astype(jnp.bfloat16)
    right_side = (jax.nn.sigmoid(projected[..., 3 * channels:]) * projected[..., 2 * channels:3 * channels] * pair_mask[..., None]).astype(jnp.bfloat16)
    product = jnp.einsum('ikc,jkc->ijc', left_side.astype(jnp.float32), right_side.astype(jnp.float32)).astype(jnp.bfloat16)
    tri_gating = jax.nn.sigmoid(jnp.dot(flat_rows, tri_gate, preferred_element_type=jnp.float32)).reshape(length, length, channels)
    product_normed = layer_norm(product.astype(jnp.float32)).astype(jnp.bfloat16)
    tri_update = tri_gating * jnp.dot(product_normed.reshape(-1, channels), tri_out, preferred_element_type=jnp.float32).reshape(length, length, channels)
    after_tri = (start_pair + tri_update).astype(jnp.bfloat16)
    second = layer_norm(after_tri.astype(jnp.float32)).astype(jnp.bfloat16)
    flat_second = second.reshape(-1, channels)
    query_gate = jnp.dot(flat_second, att_query, preferred_element_type=jnp.float32).reshape(length, length, 2 * heads_width)
    query = (query_gate[..., :heads_width] * HEAD_DIM ** (-0.5)).astype(jnp.bfloat16).reshape(length, length, HEADS, HEAD_DIM)
    gating = jax.nn.sigmoid(query_gate[..., heads_width:])
    keyval = jnp.dot(flat_second, att_kv, preferred_element_type=jnp.float32).astype(jnp.bfloat16).reshape(length, length, 2 * heads_width)
    key_heads = keyval[..., :heads_width].reshape(length, length, HEADS, HEAD_DIM)
    value_heads = keyval[..., heads_width:].reshape(length, length, HEADS, HEAD_DIM)
    tri_bias = jnp.dot(flat_second, att_bias, preferred_element_type=jnp.float32).astype(jnp.bfloat16).reshape(length, length, HEADS)
    bias_heads = jnp.transpose(tri_bias, (2, 0, 1)).astype(jnp.float32)

    def one_row(operands):
        query_row, key_row, value_row = operands
        scores = jnp.einsum('jhd,khd->hjk', query_row.astype(jnp.float32), key_row.astype(jnp.float32)) + bias_heads
        weights = (jnp.exp(scores) * living[None, None, :]).astype(jnp.bfloat16)
        totals = lax.optimization_barrier(jnp.sum(weights.astype(jnp.float32), axis=2))
        summed = jnp.einsum('hjk,khd->jhd', weights.astype(jnp.float32), value_row.astype(jnp.float32))
        return summed / jnp.transpose(totals)[:, :, None]
    attended = lax.map(one_row, (query, key_heads, value_heads))
    outgoing = (attended.reshape(length, length, heads_width) * gating).astype(jnp.bfloat16)
    result = after_tri.astype(jnp.float32) + jnp.dot(outgoing.reshape(-1, heads_width), att_out, preferred_element_type=jnp.float32).reshape(length, length, channels)
    return result.astype(jnp.bfloat16)
```

```python
import functools

import jax
import jax.numpy as jnp
from jax import lax
from jax.experimental import pallas as pl
from jax.experimental.pallas import tpu as pltpu
from jax.sharding import PartitionSpec as P

HEADS = 4
HEAD_DIM = 32


EPSILON = 1e-05


def layer_norm(values):
    average = jnp.mean(values, axis=-1, keepdims=True)
    centred = values - average
    spread = jnp.mean(centred * centred, axis=-1, keepdims=True)
    return centred * lax.rsqrt(spread + EPSILON)


def on_device(
    pair,
    chain_ids,
    residue_mask,
    chain_vec,
    tri_in,
    tri_gate,
    tri_out,
    att_query,
    att_kv,
    att_bias,
    att_out,
):
    rows, cols, channels = pair.shape
    heads_width = HEADS * HEAD_DIM
    row_start = lax.axis_index("row") * rows
    col_block = lax.axis_index(("col", "sub"))
    col_start = col_block * cols
    living = residue_mask.astype(jnp.float32)
    row_live = lax.dynamic_slice_in_dim(living, row_start, rows)
    col_live = lax.dynamic_slice_in_dim(living, col_start, cols)
    row_chain = lax.dynamic_slice_in_dim(chain_ids, row_start, rows)
    col_chain = lax.dynamic_slice_in_dim(chain_ids, col_start, cols)
    same_chain = (row_chain[:, None] == col_chain[None, :]).astype(jnp.float32)
    pair_mask = row_live[:, None] * col_live[None, :]
    start_pair = pair.astype(jnp.float32) + same_chain[:, :, None] * chain_vec
    normed = layer_norm(start_pair).astype(jnp.bfloat16)
    flat_rows = normed.reshape(rows * cols, channels)
    projected = jnp.dot(flat_rows, tri_in, preferred_element_type=jnp.float32).reshape(
        rows, cols, 4 * channels
    )
    left_side = (
        jax.nn.sigmoid(projected[..., channels : 2 * channels])
        * projected[..., :channels]
        * pair_mask[..., None]
    )
    right_side = (
        jax.nn.sigmoid(projected[..., 3 * channels :])
        * projected[..., 2 * channels : 3 * channels]
        * pair_mask[..., None]
    )
    stacked = jnp.transpose(jnp.stack([left_side, right_side]).astype(jnp.bfloat16), (0, 3, 1, 2))
    regrouped = lax.all_to_all(
        lax.all_to_all(stacked, "row", split_axis=1, concat_axis=2, tiled=True),
        ("col", "sub"),
        split_axis=2,
        concat_axis=3,
        tiled=True,
    )
    left_part = regrouped[0]
    right_part = regrouped[1]
    product = jnp.einsum(
        "cjk,cik->cji",
        right_part,
        lax.all_gather(left_part, ("col", "sub"), axis=1, tiled=True),
        preferred_element_type=jnp.float32,
    ).astype(jnp.bfloat16)
    returned = lax.all_to_all(product, "row", split_axis=2, concat_axis=0, tiled=True)
    product_pairs = jnp.transpose(returned, (2, 1, 0)).astype(jnp.float32)
    tri_gating = jax.nn.sigmoid(
        jnp.dot(flat_rows, tri_gate, preferred_element_type=jnp.float32)
    ).reshape(rows, cols, channels)
    product_normed = layer_norm(product_pairs).astype(jnp.bfloat16)
    tri_update = tri_gating * jnp.dot(
        product_normed.reshape(-1, channels), tri_out, preferred_element_type=jnp.float32
    ).reshape(rows, cols, channels)
    after_tri = (start_pair + tri_update).astype(jnp.bfloat16)
    second = layer_norm(after_tri.astype(jnp.float32)).astype(jnp.bfloat16)
    flat_second = second.reshape(-1, channels)
    query_gate = jnp.dot(flat_second, att_query, preferred_element_type=jnp.float32).reshape(
        rows, cols, 2 * heads_width
    )
    query = (
        (query_gate[..., :heads_width] * HEAD_DIM ** (-0.5))
        .astype(jnp.bfloat16)
        .reshape(rows, cols, HEADS, HEAD_DIM)
    )
    gating = jax.nn.sigmoid(query_gate[..., heads_width:])
    local_bias = (
        jnp.dot(flat_second, att_bias, preferred_element_type=jnp.float32)
        .astype(jnp.bfloat16)
        .reshape(rows, cols, HEADS)
    )
    local_bias = jnp.transpose(local_bias, (2, 0, 1))
    column_all = lax.all_gather(local_bias, "row", axis=1, tiled=True)
    bias_rows = lax.all_to_all(column_all, ("col", "sub"), split_axis=1, concat_axis=2, tiled=True)
    piece = lax.all_gather(second, ("col", "sub"), axis=1, tiled=True)
    width = piece.shape[1]
    keyval = (
        jnp.dot(piece.reshape(-1, channels), att_kv, preferred_element_type=jnp.float32)
        .astype(jnp.bfloat16)
        .reshape(rows, width, 2 * heads_width)
    )
    width = keyval.shape[1]
    key_heads = keyval[..., :heads_width].reshape(rows, width, HEADS, HEAD_DIM)
    value_heads = keyval[..., heads_width:].reshape(rows, width, HEADS, HEAD_DIM)
    scores = jnp.einsum("ijhd,ikhd->ihjk", query, key_heads, preferred_element_type=jnp.float32)
    scores = scores + bias_rows.astype(jnp.float32)[None]
    weights = (jnp.exp(scores) * living).astype(jnp.bfloat16)
    summed = jnp.einsum("ihjk,ikhd->ijhd", weights, value_heads, preferred_element_type=jnp.float32)
    totals = jnp.sum(weights.astype(jnp.float32), axis=3)
    summed, totals = (summed, totals)
    attended = summed / jnp.transpose(totals, (0, 2, 1))[..., None]
    outgoing = (attended.reshape(rows, cols, heads_width) * gating).astype(jnp.bfloat16)
    result = after_tri.astype(jnp.float32) + jnp.dot(
        outgoing.reshape(-1, heads_width), att_out, preferred_element_type=jnp.float32
    ).reshape(rows, cols, channels)
    return result.astype(jnp.bfloat16)


MESH = pl.DeviceIdType.MESH
F32, BF16 = jnp.float32, jnp.bfloat16
NT = (((1,), (1,)), ((), ()))
TN = (((0,), (0,)), ((), ()))
NN = (((1,), (0,)), ((), ()))
MASKED = -3.0e38
VMEM_LIMIT = 60 * 1024 * 1024


def gate_of(values):
    return 0.5 * jnp.tanh(0.5 * values) + 0.5


def dot(a, b, dims=NN):
    return lax.dot_general(a, b, dims, preferred_element_type=F32)


def norm_rows(values):
    average = jnp.mean(values, axis=-1, keepdims=True)
    centred = values - average
    spread = jnp.mean(centred * centred, axis=-1, keepdims=True)
    return centred * lax.rsqrt(spread + EPSILON)


def exchange(kernel_id, sizes, everyone, src_of, dst_of, x, out_shape):
    nr, nc, ns = sizes
    nq = nc * ns
    count = nr * nq if everyone else nq

    def kernel(x_ref, y_ref, send_sem, recv_sem, own_sem):
        q = lax.axis_index("col") * ns + lax.axis_index("sub")
        me = lax.axis_index("row") * nq + q if everyone else q

        def device(p):
            where = {"col": lax.rem(p, nq) // ns, "sub": lax.rem(p, ns)}
            if everyone:
                where["row"] = p // nq
            return where

        barrier = pltpu.get_barrier_semaphore()
        peers = [lax.rem(me + d, count) for d in range(1, count)]
        for p in peers:
            pl.semaphore_signal(barrier, inc=1, device_id=device(p), device_id_type=MESH)
        pl.semaphore_wait(barrier, count - 1)
        copies = []
        for d, p in enumerate(peers):
            copy = pltpu.make_async_remote_copy(
                src_ref=src_of(x_ref, p),
                dst_ref=dst_of(y_ref, me),
                send_sem=send_sem.at[d],
                recv_sem=recv_sem.at[d],
                device_id=device(p),
                device_id_type=MESH,
            )
            copy.start()
            copies.append(copy)
        own = pltpu.make_async_copy(src_of(x_ref, me), dst_of(y_ref, me), own_sem)
        own.start()
        own.wait()
        for copy in copies:
            copy.wait()

    return pl.pallas_call(
        kernel,
        out_shape=out_shape,
        in_specs=[pl.BlockSpec(memory_space=pl.ANY)],
        out_specs=pl.BlockSpec(memory_space=pl.ANY),
        scratch_shapes=[
            pltpu.SemaphoreType.DMA((count - 1,)),
            pltpu.SemaphoreType.DMA((count - 1,)),
            pltpu.SemaphoreType.DMA,
        ],
        compiler_params=pltpu.CompilerParams(collective_id=kernel_id, has_side_effects=True),
        name="exchange_%d" % kernel_id,
    )(x)


def project_kernel(row_chain, row_live, pair_ref, chain_cols, chain_vec, live_cols, weight, out_ref):
    i = pl.program_id(0)
    same = jnp.where(chain_cols[...] == row_chain[i], chain_vec[...], 0.0)
    normed = norm_rows(pair_ref[0].astype(F32) + same).astype(BF16)
    half = weight.shape[0] // 2
    projected = dot(weight[...], normed, NT)
    mask = live_cols[...] * row_live[i]
    sides = gate_of(projected[half:]) * projected[:half] * mask
    groups, wide = out_ref.shape[0], out_ref.shape[2]
    out_ref[:, 0] = sides.astype(BF16).reshape(groups, wide, sides.shape[1])


def product_kernel(count, x_ref, out_ref, *scratch):
    lanes = x_ref.shape[1] // 128
    flat, made = scratch[:lanes], scratch[lanes:]
    total = x_ref.shape[0]
    wide = 2 * count
    length = total // wide
    step = length

    @pl.loop(0, total // step)
    def _(s):
        at = pl.ds(pl.multiple_of(s * step, step), step)
        for t in range(lanes):
            flat[t][at, :] = x_ref[at, t * 128 : (t + 1) * 128].astype(F32)

    for c in range(count):
        left = [flat[t][pl.ds(c, length, stride=wide), :].astype(BF16) for t in range(lanes)]
        right = [flat[t][pl.ds(count + c, length, stride=wide), :].astype(BF16) for t in range(lanes)]
        product = dot(jnp.concatenate(left, axis=1), jnp.concatenate(right, axis=1), NT)
        for t in range(lanes):
            made[t][pl.ds(c, length, stride=count), :] = product[:, t * 128 : (t + 1) * 128]

    @pl.loop(0, out_ref.shape[0] // step)
    def _(s):
        at = pl.ds(pl.multiple_of(s * step, step), step)
        for t in range(lanes):
            out_ref[at, t * 128 : (t + 1) * 128] = made[t][at, :].astype(BF16)


def update_kernel(
    row_chain, pair_ref, prod_ref, chain_cols, chain_vec, live_cols, tri_gate, tri_out, att_bias,
    after_ref, second_ref, bias_ref,
):
    step = pl.program_id(0)
    groups, wide, length = prod_ref.shape
    per = wide // 2
    both = prod_ref[...].astype(F32)
    for u in range(2):
        i = step * 2 + u
        same = jnp.where(chain_cols[...] == row_chain[i], chain_vec[...], 0.0)
        start = pair_ref[u].astype(F32) + same
        normed = norm_rows(start).astype(BF16)
        gating = gate_of(dot(normed, tri_gate[...]))
        product = both[:, u * per : (u + 1) * per, :].reshape(groups * per, length)
        average = jnp.mean(product, axis=0, keepdims=True)
        centred = product - average
        spread = jnp.mean(centred * centred, axis=0, keepdims=True)
        product_normed = (centred * lax.rsqrt(spread + EPSILON)).astype(BF16)
        after = (start + gating * dot(product_normed, tri_out[...], TN)).astype(BF16)
        second = norm_rows(after.astype(F32)).astype(BF16)
        after_ref[u] = after
        second_ref[u] = second
        bias = dot(att_bias[...], second, NT)
        bias = jnp.where(live_cols[...] > 0.0, bias, MASKED)
        for h in range(HEADS):
            bias_ref[h, pl.ds(i, 1), :] = bias[h : h + 1, :]


def attend_kernel(second_ref, after_ref, bias_ref, att_query, att_kv, att_out, out_ref):
    width = HEADS * HEAD_DIM
    second = second_ref[0]
    query_gate = dot(second, att_query[...])
    query = (query_gate[:, :width] * HEAD_DIM ** (-0.5)).astype(BF16)
    gating = gate_of(query_gate[:, width:])
    keyval = dot(second, att_kv[...]).astype(BF16)
    key, value = keyval[:, :width], keyval[:, width:]
    head = lax.broadcasted_iota(jnp.int32, value.shape, 1) // HEAD_DIM
    summed = None
    for h in range(HEADS):
        mine = (head == h).astype(BF16)
        scores = dot(query * mine, key, NT) + bias_ref[h]
        weights = jnp.exp(scores).astype(BF16)
        part = dot(weights, jnp.concatenate([value * mine, mine], axis=1))
        summed = part if summed is None else summed + part
    attended = summed[:, :width] / summed[:, width:]
    outgoing = (attended * gating).astype(BF16)
    result = after_ref[0].astype(F32) + dot(outgoing, att_out[...])
    out_ref[0] = result.astype(BF16)


def by_rows(
    sizes,
    pair,
    chain_ids,
    residue_mask,
    chain_vec,
    tri_in,
    tri_gate,
    tri_out,
    att_query,
    att_kv,
    att_bias,
    att_out,
):
    nr, nc, ns = sizes
    nq = nc * ns
    groups = nr * nq
    rows, cols, channels = pair.shape
    own = rows // nq
    length = cols * nq
    per = channels // groups
    me = (lax.axis_index("row") * nc + lax.axis_index("col")) * ns + lax.axis_index("sub")
    living = residue_mask.astype(F32)
    row_chain = lax.dynamic_slice_in_dim(chain_ids, me * own, own)
    row_live = lax.dynamic_slice_in_dim(living, me * own, own)
    chain_cols = jnp.broadcast_to(chain_ids[:, None], (length, channels))
    live_cols = living[None, :]
    chain_row = chain_vec[None, :]

    def interleave(a, b):
        both = jnp.stack([a.T.reshape(groups, per, channels), b.T.reshape(groups, per, channels)], axis=1)
        return both.reshape(2 * channels, channels)

    quarter = [tri_in[:, n * channels : (n + 1) * channels] for n in range(4)]
    weight = jnp.concatenate([interleave(quarter[0], quarter[2]), interleave(quarter[1], quarter[3])])
    bias_weight = jnp.pad(att_bias.T, ((0, 8 - HEADS), (0, 0)))

    pair_rows = exchange(
        1, sizes, False,
        lambda x, p: x.at[pl.ds(p * own, own)],
        lambda y, m: y.at[:, pl.ds(m * cols, cols), :],
        pair,
        jax.ShapeDtypeStruct((own, length, channels), BF16),
    )
    smem = pl.BlockSpec(memory_space=pltpu.SMEM)

    def whole(*shape):
        return pl.BlockSpec(shape, lambda s: (0,) * len(shape))

    def row_block(n):
        return pl.BlockSpec((n, length, channels), lambda s: (s, 0, 0))

    params = pltpu.CompilerParams(vmem_limit_bytes=VMEM_LIMIT)
    sides = pl.pallas_call(
        project_kernel,
        grid=(own,),
        in_specs=[smem, smem, row_block(1), whole(length, channels), whole(1, channels),
                  whole(1, length), whole(4 * channels, channels)],
        out_specs=pl.BlockSpec((groups, 1, 2 * per, length), lambda s: (0, s, 0, 0)),
        out_shape=jax.ShapeDtypeStruct((groups, own, 2 * per, length), BF16),
        compiler_params=params,
        name="project",
    )(row_chain, row_live, pair_rows, chain_cols, chain_row, live_cols, weight)
    regrouped = exchange(
        2, sizes, True, lambda x, p: x.at[p], lambda y, m: y.at[m], sides,
        jax.ShapeDtypeStruct(sides.shape, BF16),
    )
    lanes = length // 128
    product = pl.pallas_call(
        functools.partial(product_kernel, per),
        out_shape=jax.ShapeDtypeStruct((length * per, length), BF16),
        in_specs=[pl.BlockSpec(memory_space=pltpu.VMEM)],
        out_specs=pl.BlockSpec(memory_space=pltpu.VMEM),
        scratch_shapes=[pltpu.VMEM((length * 2 * per, 128), F32)] * lanes
        + [pltpu.VMEM((length * per, 128), F32)] * lanes,
        compiler_params=params,
        name="product",
    )(regrouped.reshape(length * 2 * per, length))
    product = product.reshape(groups, own * per, length)
    returned = exchange(
        3, sizes, True, lambda x, p: x.at[p], lambda y, m: y.at[m], product,
        jax.ShapeDtypeStruct(product.shape, BF16),
    )
    row_shape = jax.ShapeDtypeStruct((own, length, channels), BF16)
    after, second, bias = pl.pallas_call(
        update_kernel,
        grid=(own // 2,),
        in_specs=[smem, row_block(2), pl.BlockSpec((groups, 2 * per, length), lambda s: (0, s, 0)),
                  whole(length, channels), whole(1, channels), whole(1, length),
                  whole(channels, channels), whole(channels, channels), whole(8, channels)],
        out_specs=[row_block(2), row_block(2), whole(HEADS, own, length)],
        out_shape=[row_shape, row_shape, jax.ShapeDtypeStruct((HEADS, own, length), F32)],
        compiler_params=params,
        name="update",
    )(row_chain, pair_rows, returned, chain_cols, chain_row, live_cols, tri_gate, tri_out, bias_weight)
    bias = bias.astype(BF16).reshape(HEADS * own, length)
    bias_all = exchange(
        4, sizes, True, lambda x, p: x, lambda y, m: y.at[m], bias,
        jax.ShapeDtypeStruct((groups, HEADS * own, length), BF16),
    )
    bias_all = jnp.transpose(bias_all.reshape(groups, HEADS, own, length), (1, 0, 2, 3))
    bias_all = bias_all.reshape(HEADS, length, length).astype(F32)
    out_rows = pl.pallas_call(
        attend_kernel,
        grid=(own,),
        in_specs=[row_block(1), row_block(1), whole(HEADS, length, length),
                  whole(channels, 2 * channels), whole(channels, 2 * channels), whole(channels, channels)],
        out_specs=row_block(1),
        out_shape=row_shape,
        compiler_params=params,
        name="attend",
    )(second, after, bias_all, att_query, att_kv, att_out)
    return exchange(
        5, sizes, False,
        lambda x, p: x.at[:, pl.ds(p * cols, cols), :],
        lambda y, m: y.at[pl.ds(m * own, own)],
        out_rows,
        jax.ShapeDtypeStruct((rows, cols, channels), BF16),
    )


def device_program(sizes, pair, *rest):
    rows, cols, channels = pair.shape
    nr, nc, ns = sizes
    nq = nc * ns
    length = cols * nq
    fits = (
        rows % (2 * nq) == 0
        and (rows // nq) % 8 == 0
        and cols % 16 == 0
        and channels == 128
        and channels == 8 * nr * nq
        and length % 128 == 0
        and length == rows * nr
    )
    if fits:
        return by_rows(sizes, pair, *rest)
    return on_device(pair, *rest)


def solution(mesh):
    sizes = tuple(mesh.shape[name] for name in ("row", "col", "sub"))
    return jax.shard_map(
        functools.partial(device_program, sizes),
        mesh=mesh,
        in_specs=(
            P(("grp", "row"), ("col", "sub"), None),
            P("grp"),
            P("grp"),
            P(),
            P(),
            P(),
            P(),
            P(),
            P(),
            P(),
            P(),
        ),
        out_specs=P(("grp", "row"), ("col", "sub"), None),
        check_vma=False,
    )
```

```python
import functools

import jax
import jax.numpy as jnp
from jax import lax
from jax.experimental import pallas as pl
from jax.experimental.pallas import tpu as pltpu
from jax.sharding import PartitionSpec as P

HEADS = 4
HEAD_DIM = 32


EPSILON = 1e-05


def layer_norm(values):
    average = jnp.mean(values, axis=-1, keepdims=True)
    centred = values - average
    spread = jnp.mean(centred * centred, axis=-1, keepdims=True)
    return centred * lax.rsqrt(spread + EPSILON)


def on_device(
    pair,
    chain_ids,
    residue_mask,
    chain_vec,
    tri_in,
    tri_gate,
    tri_out,
    att_query,
    att_kv,
    att_bias,
    att_out,
):
    rows, cols, channels = pair.shape
    heads_width = HEADS * HEAD_DIM
    row_start = lax.axis_index("row") * rows
    col_block = lax.axis_index(("col", "sub"))
    col_start = col_block * cols
    living = residue_mask.astype(jnp.float32)
    row_live = lax.dynamic_slice_in_dim(living, row_start, rows)
    col_live = lax.dynamic_slice_in_dim(living, col_start, cols)
    row_chain = lax.dynamic_slice_in_dim(chain_ids, row_start, rows)
    col_chain = lax.dynamic_slice_in_dim(chain_ids, col_start, cols)
    same_chain = (row_chain[:, None] == col_chain[None, :]).astype(jnp.float32)
    pair_mask = row_live[:, None] * col_live[None, :]
    start_pair = pair.astype(jnp.float32) + same_chain[:, :, None] * chain_vec
    normed = layer_norm(start_pair).astype(jnp.bfloat16)
    flat_rows = normed.reshape(rows * cols, channels)
    projected = jnp.dot(flat_rows, tri_in, preferred_element_type=jnp.float32).reshape(
        rows, cols, 4 * channels
    )
    left_side = (
        jax.nn.sigmoid(projected[..., channels : 2 * channels])
        * projected[..., :channels]
        * pair_mask[..., None]
    )
    right_side = (
        jax.nn.sigmoid(projected[..., 3 * channels :])
        * projected[..., 2 * channels : 3 * channels]
        * pair_mask[..., None]
    )
    stacked = jnp.transpose(jnp.stack([left_side, right_side]).astype(jnp.bfloat16), (0, 3, 1, 2))
    regrouped = lax.all_to_all(
        lax.all_to_all(stacked, "row", split_axis=1, concat_axis=2, tiled=True),
        ("col", "sub"),
        split_axis=2,
        concat_axis=3,
        tiled=True,
    )
    left_part = regrouped[0]
    right_part = regrouped[1]
    product = jnp.einsum(
        "cjk,cik->cji",
        right_part,
        lax.all_gather(left_part, ("col", "sub"), axis=1, tiled=True),
        preferred_element_type=jnp.float32,
    ).astype(jnp.bfloat16)
    returned = lax.all_to_all(product, "row", split_axis=2, concat_axis=0, tiled=True)
    product_pairs = jnp.transpose(returned, (2, 1, 0)).astype(jnp.float32)
    tri_gating = jax.nn.sigmoid(
        jnp.dot(flat_rows, tri_gate, preferred_element_type=jnp.float32)
    ).reshape(rows, cols, channels)
    product_normed = layer_norm(product_pairs).astype(jnp.bfloat16)
    tri_update = tri_gating * jnp.dot(
        product_normed.reshape(-1, channels), tri_out, preferred_element_type=jnp.float32
    ).reshape(rows, cols, channels)
    after_tri = (start_pair + tri_update).astype(jnp.bfloat16)
    second = layer_norm(after_tri.astype(jnp.float32)).astype(jnp.bfloat16)
    flat_second = second.reshape(-1, channels)
    query_gate = jnp.dot(flat_second, att_query, preferred_element_type=jnp.float32).reshape(
        rows, cols, 2 * heads_width
    )
    query = (
        (query_gate[..., :heads_width] * HEAD_DIM ** (-0.5))
        .astype(jnp.bfloat16)
        .reshape(rows, cols, HEADS, HEAD_DIM)
    )
    gating = jax.nn.sigmoid(query_gate[..., heads_width:])
    local_bias = (
        jnp.dot(flat_second, att_bias, preferred_element_type=jnp.float32)
        .astype(jnp.bfloat16)
        .reshape(rows, cols, HEADS)
    )
    local_bias = jnp.transpose(local_bias, (2, 0, 1))
    column_all = lax.all_gather(local_bias, "row", axis=1, tiled=True)
    bias_rows = lax.all_to_all(column_all, ("col", "sub"), split_axis=1, concat_axis=2, tiled=True)
    piece = lax.all_gather(second, ("col", "sub"), axis=1, tiled=True)
    width = piece.shape[1]
    keyval = (
        jnp.dot(piece.reshape(-1, channels), att_kv, preferred_element_type=jnp.float32)
        .astype(jnp.bfloat16)
        .reshape(rows, width, 2 * heads_width)
    )
    width = keyval.shape[1]
    key_heads = keyval[..., :heads_width].reshape(rows, width, HEADS, HEAD_DIM)
    value_heads = keyval[..., heads_width:].reshape(rows, width, HEADS, HEAD_DIM)
    scores = jnp.einsum("ijhd,ikhd->ihjk", query, key_heads, preferred_element_type=jnp.float32)
    scores = scores + bias_rows.astype(jnp.float32)[None]
    weights = (jnp.exp(scores) * living).astype(jnp.bfloat16)
    summed = jnp.einsum("ihjk,ikhd->ijhd", weights, value_heads, preferred_element_type=jnp.float32)
    totals = jnp.sum(weights.astype(jnp.float32), axis=3)
    summed, totals = (summed, totals)
    attended = summed / jnp.transpose(totals, (0, 2, 1))[..., None]
    outgoing = (attended.reshape(rows, cols, heads_width) * gating).astype(jnp.bfloat16)
    result = after_tri.astype(jnp.float32) + jnp.dot(
        outgoing.reshape(-1, heads_width), att_out, preferred_element_type=jnp.float32
    ).reshape(rows, cols, channels)
    return result.astype(jnp.bfloat16)


MESH = pl.DeviceIdType.MESH
F32, BF16 = jnp.float32, jnp.bfloat16
NT = (((1,), (1,)), ((), ()))
TN = (((0,), (0,)), ((), ()))
NN = (((1,), (0,)), ((), ()))
MASKED = -3.0e38
VMEM_LIMIT = 60 * 1024 * 1024


def gate_of(values):
    return 0.5 * jnp.tanh(0.5 * values) + 0.5


def dot(a, b, dims=NN):
    return lax.dot_general(a, b, dims, preferred_element_type=F32)


def norm_rows(values):
    average = jnp.mean(values, axis=-1, keepdims=True)
    centred = values - average
    spread = jnp.mean(centred * centred, axis=-1, keepdims=True)
    return centred * lax.rsqrt(spread + EPSILON)


CHUNK = 4


def position(sizes):
    nr, nc, ns = sizes
    r = lax.axis_index("row")
    q = lax.axis_index("col") * ns + lax.axis_index("sub")

    def device(row, place):
        return {"row": row, "col": place // ns, "sub": lax.rem(place, ns)}

    return r, q, device


def peers_of(sizes):
    nr, nc, ns = sizes
    nq = nc * ns
    r, q, device = position(sizes)
    found = []
    for d in range(1, nr * nq):
        dr, dq = d // nq, d % nq
        row, place = lax.rem(r + dr, nr), lax.rem(q + dq, nq)
        found.append((row * nq + place, device(row, place)))
    return found


def meet(devices):
    barrier = pltpu.get_barrier_semaphore()
    for where in devices:
        pl.semaphore_signal(barrier, inc=1, device_id=where, device_id_type=MESH)
    pl.semaphore_wait(barrier, len(devices))


def send(src, dst, send_sem, recv_sem, where):
    copy = pltpu.make_async_remote_copy(
        src_ref=src, dst_ref=dst, send_sem=send_sem, recv_sem=recv_sem,
        device_id=where, device_id_type=MESH,
    )
    copy.start()
    return copy


def project_kernel(
    sizes, row_chain, row_live, chain_cols, chain_vec, live_cols, weight, pair_ref,
    rows_ref, grouped_ref, sides, in_send, in_recv, in_own, out_send, out_recv, out_own,
):
    nr, nc, ns = sizes
    nq = nc * ns
    r, q, device = position(sizes)
    me = r * nq + q
    groups, own, wide, length = sides.shape
    cols = length // nq
    chunks = own // CHUNK
    half = weight.shape[0] // 2
    peers = peers_of(sizes)
    meet([where for _, where in peers])
    arriving = []
    for n in range(chunks):
        some = pl.ds(n * CHUNK, CHUNK)
        here = pl.ds(q * cols, cols)
        now = []
        for d in range(1, nq):
            p = lax.rem(q + d, nq)
            now.append(send(
                pair_ref.at[pl.ds(p * own + n * CHUNK, CHUNK)], rows_ref.at[some, here, :],
                in_send.at[n, d - 1], in_recv.at[n, d - 1], device(r, p),
            ))
        mine = pltpu.make_async_copy(
            pair_ref.at[pl.ds(q * own + n * CHUNK, CHUNK)], rows_ref.at[some, here, :], in_own.at[n]
        )
        mine.start()
        arriving.append((now, mine))
    leaving = []
    for n in range(chunks):
        now, mine = arriving[n]
        mine.wait()
        for copy in now:
            copy.wait_recv()

        @pl.loop(n * CHUNK, (n + 1) * CHUNK)
        def _(i):
            same = jnp.where(chain_cols[...] == row_chain[i], chain_vec[...], 0.0)
            normed = norm_rows(rows_ref[i].astype(F32) + same).astype(BF16)
            projected = dot(weight[...], normed, NT)
            mask = live_cols[...] * row_live[i]
            both = gate_of(projected[half:]) * projected[:half] * mask
            sides[:, i] = both.astype(BF16).reshape(groups, wide, length)

        some = pl.ds(n * CHUNK, CHUNK)
        for d, (p, where) in enumerate(peers):
            leaving.append(send(
                sides.at[p, some], grouped_ref.at[me, some], out_send.at[n, d], out_recv.at[n, d], where
            ))
        mine = pltpu.make_async_copy(sides.at[me, some], grouped_ref.at[me, some], out_own.at[n])
        mine.start()
        leaving.append(mine)
    for now, _ in arriving:
        for copy in now:
            copy.wait_send()
    for copy in leaving:
        copy.wait()


def product_kernel(count, x_ref, out_ref, *scratch):
    lanes = x_ref.shape[1] // 128
    flat, made = scratch[:lanes], scratch[lanes:]
    total = x_ref.shape[0]
    wide = 2 * count
    length = total // wide
    step = length

    @pl.loop(0, total // step)
    def _(s):
        at = pl.ds(pl.multiple_of(s * step, step), step)
        for t in range(lanes):
            flat[t][at, :] = x_ref[at, t * 128 : (t + 1) * 128].astype(F32)

    for c in range(count):
        left = [flat[t][pl.ds(c, length, stride=wide), :].astype(BF16) for t in range(lanes)]
        right = [flat[t][pl.ds(count + c, length, stride=wide), :].astype(BF16) for t in range(lanes)]
        product = dot(jnp.concatenate(left, axis=1), jnp.concatenate(right, axis=1), NT)
        for t in range(lanes):
            made[t][pl.ds(c, length, stride=count), :] = product[:, t * 128 : (t + 1) * 128]

    @pl.loop(0, out_ref.shape[0] // step)
    def _(s):
        at = pl.ds(pl.multiple_of(s * step, step), step)
        for t in range(lanes):
            out_ref[at, t * 128 : (t + 1) * 128] = made[t][at, :].astype(BF16)


def update_kernel(
    sizes, row_chain, pair_ref, prod_ref, chain_cols, chain_vec, live_cols, tri_gate, tri_out, att_bias,
    after_ref, second_ref, gathered, landed, bias_ref, bias_out,
    in_send, in_recv, in_own, row_send, row_recv, col_send, col_recv, sub_send, sub_recv, own_sem,
):
    nr, nc, ns = sizes
    nq = nc * ns
    r, q, device = position(sizes)
    c, u = lax.axis_index("col"), lax.axis_index("sub")
    me = r * nq + q
    groups, tall, length = landed.shape
    own = pair_ref.shape[0]
    per = tall // own
    chunks = own // CHUNK
    peers = peers_of(sizes)
    meet([where for _, where in peers])
    arriving = []
    for n in range(chunks):
        some = pl.ds(n * CHUNK * per, CHUNK * per)
        now = [
            send(prod_ref.at[p, some], landed.at[me, some], in_send.at[n, d], in_recv.at[n, d], where)
            for d, (p, where) in enumerate(peers)
        ]
        mine = pltpu.make_async_copy(prod_ref.at[me, some], landed.at[me, some], in_own.at[n])
        mine.start()
        arriving.append((now, mine))
    for n in range(chunks):
        now, mine = arriving[n]
        mine.wait()
        for copy in now:
            copy.wait_recv()

        @pl.loop(n * CHUNK // 2, (n + 1) * CHUNK // 2)
        def _(step):
            at = pl.ds(pl.multiple_of(step * 2 * per, 2 * per), 2 * per)
            both = landed[:, at, :].astype(F32)
            for v in range(2):
                i = step * 2 + v
                same = jnp.where(chain_cols[...] == row_chain[i], chain_vec[...], 0.0)
                start = pair_ref[i].astype(F32) + same
                normed = norm_rows(start).astype(BF16)
                gating = gate_of(dot(normed, tri_gate[...]))
                product = both[:, v * per : (v + 1) * per, :].reshape(groups * per, length)
                average = jnp.mean(product, axis=0, keepdims=True)
                centred = product - average
                spread = jnp.mean(centred * centred, axis=0, keepdims=True)
                product_normed = (centred * lax.rsqrt(spread + EPSILON)).astype(BF16)
                after = (start + gating * dot(product_normed, tri_out[...], TN)).astype(BF16)
                second = norm_rows(after.astype(F32)).astype(BF16)
                after_ref[i] = after
                second_ref[i] = second
                bias = dot(att_bias[...], second, NT)
                bias = jnp.where(live_cols[...] > 0.0, bias, MASKED)
                for h in range(HEADS):
                    bias_ref[pl.ds(h * own + i, 1), :] = bias[h : h + 1, :]

    bias_out[...] = bias_ref[...].astype(BF16)
    mine = pltpu.make_async_copy(bias_out, gathered.at[q, r], own_sem)
    mine.start()
    hops = []
    for d in range(1, nr):
        hops.append(send(
            bias_out, gathered.at[q, r], row_send.at[d - 1], row_recv.at[d - 1],
            device(lax.rem(r + d, nr), q),
        ))
    mine.wait()
    for copy in hops:
        copy.wait_recv()
    across = []
    for d in range(1, nc):
        across.append(send(
            gathered.at[q], gathered.at[q], col_send.at[d - 1], col_recv.at[d - 1],
            device(r, lax.rem(c + d, nc) * ns + u),
        ))
    last = []

    def pass_on(e):
        source = lax.rem(c + nc - e, nc) * ns + u
        for d in range(1, ns):
            last.append(send(
                gathered.at[source], gathered.at[source], sub_send.at[e, d - 1], sub_recv.at[e, d - 1],
                device(r, c * ns + lax.rem(u + d, ns)),
            ))

    pass_on(0)
    for e, copy in enumerate(across):
        copy.wait_recv()
        pass_on(e + 1)
    for copy in last:
        copy.wait()
    for copy in hops + across:
        copy.wait_send()
    for now, _ in arriving:
        for copy in now:
            copy.wait_send()


def attend_kernel(
    sizes, second_ref, after_ref, bias_ref, att_query, att_kv, att_out,
    out_ref, made, out_send, out_recv, out_own,
):
    nr, nc, ns = sizes
    nq = nc * ns
    r, q, device = position(sizes)
    own, length, width = made.shape
    cols = length // nq
    others = [lax.rem(q + d, nq) for d in range(1, nq)]
    meet([device(r, p) for p in others])
    head = lax.broadcasted_iota(jnp.int32, (length, width), 1) // HEAD_DIM
    leaving = []
    for n in range(own // CHUNK):

        @pl.loop(n * CHUNK, (n + 1) * CHUNK)
        def _(i):
            second = second_ref[i]
            query_gate = dot(second, att_query[...])
            query = (query_gate[:, :width] * HEAD_DIM ** (-0.5)).astype(BF16)
            gating = gate_of(query_gate[:, width:])
            keyval = dot(second, att_kv[...]).astype(BF16)
            key, value = keyval[:, :width], keyval[:, width:]
            summed = None
            for h in range(HEADS):
                mine = (head == h).astype(BF16)
                scores = dot(query * mine, key, NT) + bias_ref[h]
                weights = jnp.exp(scores).astype(BF16)
                part = dot(weights, jnp.concatenate([value * mine, mine], axis=1))
                summed = part if summed is None else summed + part
            attended = summed[:, :width] / summed[:, width:]
            outgoing = (attended * gating).astype(BF16)
            result = after_ref[i].astype(F32) + dot(outgoing, att_out[...])
            made[i] = result.astype(BF16)

        some = pl.ds(n * CHUNK, CHUNK)
        to = pl.ds(q * own + n * CHUNK, CHUNK)
        for d, p in enumerate(others):
            leaving.append(send(
                made.at[some, pl.ds(p * cols, cols), :], out_ref.at[to],
                out_send.at[n, d], out_recv.at[n, d], device(r, p),
            ))
        mine = pltpu.make_async_copy(made.at[some, pl.ds(q * cols, cols), :], out_ref.at[to], out_own.at[n])
        mine.start()
        leaving.append(mine)
    for copy in leaving:
        copy.wait()


def by_rows(
    sizes,
    pair,
    chain_ids,
    residue_mask,
    chain_vec,
    tri_in,
    tri_gate,
    tri_out,
    att_query,
    att_kv,
    att_bias,
    att_out,
):
    nr, nc, ns = sizes
    nq = nc * ns
    groups = nr * nq
    rows, cols, channels = pair.shape
    own = rows // nq
    length = cols * nq
    per = channels // groups
    me = (lax.axis_index("row") * nc + lax.axis_index("col")) * ns + lax.axis_index("sub")
    living = residue_mask.astype(F32)
    row_chain = lax.dynamic_slice_in_dim(chain_ids, me * own, own)
    row_live = lax.dynamic_slice_in_dim(living, me * own, own)
    chain_cols = jnp.broadcast_to(chain_ids[:, None], (length, channels))
    live_cols = living[None, :]
    chain_row = chain_vec[None, :]

    def interleave(a, b):
        both = jnp.stack([a.T.reshape(groups, per, channels), b.T.reshape(groups, per, channels)], axis=1)
        return both.reshape(2 * channels, channels)

    quarter = [tri_in[:, n * channels : (n + 1) * channels] for n in range(4)]
    weight = jnp.concatenate([interleave(quarter[0], quarter[2]), interleave(quarter[1], quarter[3])])
    bias_weight = jnp.pad(att_bias.T, ((0, 8 - HEADS), (0, 0)))

    chunks = own // CHUNK
    smem = pl.BlockSpec(memory_space=pltpu.SMEM)
    vmem = pl.BlockSpec(memory_space=pltpu.VMEM)
    anywhere = pl.BlockSpec(memory_space=pl.ANY)
    dma = pltpu.SemaphoreType.DMA
    row_shape = jax.ShapeDtypeStruct((own, length, channels), BF16)

    def params(n):
        return pltpu.CompilerParams(collective_id=n, has_side_effects=True, vmem_limit_bytes=VMEM_LIMIT)

    side_shape = (groups, own, 2 * per, length)
    pair_rows, regrouped = pl.pallas_call(
        functools.partial(project_kernel, sizes),
        in_specs=[smem, smem, vmem, vmem, vmem, vmem, anywhere],
        out_specs=[vmem, anywhere],
        out_shape=[row_shape, jax.ShapeDtypeStruct(side_shape, BF16)],
        scratch_shapes=[
            pltpu.VMEM(side_shape, BF16),
            dma((chunks, nq - 1)), dma((chunks, nq - 1)), dma((chunks,)),
            dma((chunks, groups - 1)), dma((chunks, groups - 1)), dma((chunks,)),
        ],
        compiler_params=params(1),
        name="project",
    )(row_chain, row_live, chain_cols, chain_row, live_cols, weight, pair)
    lanes = length // 128
    product = pl.pallas_call(
        functools.partial(product_kernel, per),
        out_shape=jax.ShapeDtypeStruct((length * per, length), BF16),
        in_specs=[vmem],
        out_specs=vmem,
        scratch_shapes=[pltpu.VMEM((length * 2 * per, 128), F32)] * lanes
        + [pltpu.VMEM((length * per, 128), F32)] * lanes,
        compiler_params=pltpu.CompilerParams(vmem_limit_bytes=VMEM_LIMIT),
        name="product",
    )(regrouped.reshape(length * 2 * per, length))
    product = product.reshape(groups, own * per, length)
    tall = HEADS * own
    after, second, bias_all = pl.pallas_call(
        functools.partial(update_kernel, sizes),
        in_specs=[smem, vmem, anywhere, vmem, vmem, vmem, vmem, vmem, vmem],
        out_specs=[vmem, vmem, vmem],
        out_shape=[row_shape, row_shape, jax.ShapeDtypeStruct((nq, nr, tall, length), BF16)],
        scratch_shapes=[
            pltpu.VMEM(product.shape, BF16), pltpu.VMEM((tall, length), F32), pltpu.VMEM((tall, length), BF16),
            dma((chunks, groups - 1)), dma((chunks, groups - 1)), dma((chunks,)),
            dma((max(nr - 1, 1),)), dma((max(nr - 1, 1),)),
            dma((max(nc - 1, 1),)), dma((max(nc - 1, 1),)),
            dma((nc, max(ns - 1, 1))), dma((nc, max(ns - 1, 1))), dma,
        ],
        compiler_params=params(2),
        name="update",
    )(row_chain, pair_rows, product, chain_cols, chain_row, live_cols, tri_gate, tri_out, bias_weight)
    bias_all = jnp.transpose(bias_all.reshape(nq, nr, HEADS, own, length), (2, 1, 0, 3, 4))
    bias_all = bias_all.reshape(HEADS, length, length).astype(F32)
    return pl.pallas_call(
        functools.partial(attend_kernel, sizes),
        in_specs=[vmem] * 6,
        out_specs=anywhere,
        out_shape=jax.ShapeDtypeStruct((rows, cols, channels), BF16),
        scratch_shapes=[
            pltpu.VMEM(row_shape.shape, BF16),
            dma((chunks, nq - 1)), dma((chunks, nq - 1)), dma((chunks,)),
        ],
        compiler_params=params(3),
        name="attend",
    )(second, after, bias_all, att_query, att_kv, att_out)


def device_program(sizes, pair, *rest):
    rows, cols, channels = pair.shape
    nr, nc, ns = sizes
    nq = nc * ns
    length = cols * nq
    fits = (
        rows % (2 * nq) == 0
        and (rows // nq) % 8 == 0
        and cols % 16 == 0
        and channels == 128
        and channels == 8 * nr * nq
        and length % 128 == 0
        and length == rows * nr
    )
    if fits:
        return by_rows(sizes, pair, *rest)
    return on_device(pair, *rest)


def solution(mesh):
    sizes = tuple(mesh.shape[name] for name in ("row", "col", "sub"))
    return jax.shard_map(
        functools.partial(device_program, sizes),
        mesh=mesh,
        in_specs=(
            P(("grp", "row"), ("col", "sub"), None),
            P("grp"),
            P("grp"),
            P(),
            P(),
            P(),
            P(),
            P(),
            P(),
            P(),
            P(),
        ),
        out_specs=P(("grp", "row"), ("col", "sub"), None),
        check_vma=False,
    )
```

```python
import functools

import jax
import jax.numpy as jnp
from jax import lax
from jax.experimental import pallas as pl
from jax.experimental.pallas import tpu as pltpu
from jax.sharding import PartitionSpec as P

HEADS = 4
HEAD_DIM = 32


EPSILON = 1e-05


def layer_norm(values):
    average = jnp.mean(values, axis=-1, keepdims=True)
    centred = values - average
    spread = jnp.mean(centred * centred, axis=-1, keepdims=True)
    return centred * lax.rsqrt(spread + EPSILON)


def on_device(
    pair,
    chain_ids,
    residue_mask,
    chain_vec,
    tri_in,
    tri_gate,
    tri_out,
    att_query,
    att_kv,
    att_bias,
    att_out,
):
    rows, cols, channels = pair.shape
    heads_width = HEADS * HEAD_DIM
    row_start = lax.axis_index("row") * rows
    col_block = lax.axis_index(("col", "sub"))
    col_start = col_block * cols
    living = residue_mask.astype(jnp.float32)
    row_live = lax.dynamic_slice_in_dim(living, row_start, rows)
    col_live = lax.dynamic_slice_in_dim(living, col_start, cols)
    row_chain = lax.dynamic_slice_in_dim(chain_ids, row_start, rows)
    col_chain = lax.dynamic_slice_in_dim(chain_ids, col_start, cols)
    same_chain = (row_chain[:, None] == col_chain[None, :]).astype(jnp.float32)
    pair_mask = row_live[:, None] * col_live[None, :]
    start_pair = pair.astype(jnp.float32) + same_chain[:, :, None] * chain_vec
    normed = layer_norm(start_pair).astype(jnp.bfloat16)
    flat_rows = normed.reshape(rows * cols, channels)
    projected = jnp.dot(flat_rows, tri_in, preferred_element_type=jnp.float32).reshape(
        rows, cols, 4 * channels
    )
    left_side = (
        jax.nn.sigmoid(projected[..., channels : 2 * channels])
        * projected[..., :channels]
        * pair_mask[..., None]
    )
    right_side = (
        jax.nn.sigmoid(projected[..., 3 * channels :])
        * projected[..., 2 * channels : 3 * channels]
        * pair_mask[..., None]
    )
    stacked = jnp.transpose(jnp.stack([left_side, right_side]).astype(jnp.bfloat16), (0, 3, 1, 2))
    regrouped = lax.all_to_all(
        lax.all_to_all(stacked, "row", split_axis=1, concat_axis=2, tiled=True),
        ("col", "sub"),
        split_axis=2,
        concat_axis=3,
        tiled=True,
    )
    left_part = regrouped[0]
    right_part = regrouped[1]
    product = jnp.einsum(
        "cjk,cik->cji",
        right_part,
        lax.all_gather(left_part, ("col", "sub"), axis=1, tiled=True),
        preferred_element_type=jnp.float32,
    ).astype(jnp.bfloat16)
    returned = lax.all_to_all(product, "row", split_axis=2, concat_axis=0, tiled=True)
    product_pairs = jnp.transpose(returned, (2, 1, 0)).astype(jnp.float32)
    tri_gating = jax.nn.sigmoid(
        jnp.dot(flat_rows, tri_gate, preferred_element_type=jnp.float32)
    ).reshape(rows, cols, channels)
    product_normed = layer_norm(product_pairs).astype(jnp.bfloat16)
    tri_update = tri_gating * jnp.dot(
        product_normed.reshape(-1, channels), tri_out, preferred_element_type=jnp.float32
    ).reshape(rows, cols, channels)
    after_tri = (start_pair + tri_update).astype(jnp.bfloat16)
    second = layer_norm(after_tri.astype(jnp.float32)).astype(jnp.bfloat16)
    flat_second = second.reshape(-1, channels)
    query_gate = jnp.dot(flat_second, att_query, preferred_element_type=jnp.float32).reshape(
        rows, cols, 2 * heads_width
    )
    query = (
        (query_gate[..., :heads_width] * HEAD_DIM ** (-0.5))
        .astype(jnp.bfloat16)
        .reshape(rows, cols, HEADS, HEAD_DIM)
    )
    gating = jax.nn.sigmoid(query_gate[..., heads_width:])
    local_bias = (
        jnp.dot(flat_second, att_bias, preferred_element_type=jnp.float32)
        .astype(jnp.bfloat16)
        .reshape(rows, cols, HEADS)
    )
    local_bias = jnp.transpose(local_bias, (2, 0, 1))
    column_all = lax.all_gather(local_bias, "row", axis=1, tiled=True)
    bias_rows = lax.all_to_all(column_all, ("col", "sub"), split_axis=1, concat_axis=2, tiled=True)
    piece = lax.all_gather(second, ("col", "sub"), axis=1, tiled=True)
    width = piece.shape[1]
    keyval = (
        jnp.dot(piece.reshape(-1, channels), att_kv, preferred_element_type=jnp.float32)
        .astype(jnp.bfloat16)
        .reshape(rows, width, 2 * heads_width)
    )
    width = keyval.shape[1]
    key_heads = keyval[..., :heads_width].reshape(rows, width, HEADS, HEAD_DIM)
    value_heads = keyval[..., heads_width:].reshape(rows, width, HEADS, HEAD_DIM)
    scores = jnp.einsum("ijhd,ikhd->ihjk", query, key_heads, preferred_element_type=jnp.float32)
    scores = scores + bias_rows.astype(jnp.float32)[None]
    weights = (jnp.exp(scores) * living).astype(jnp.bfloat16)
    summed = jnp.einsum("ihjk,ikhd->ijhd", weights, value_heads, preferred_element_type=jnp.float32)
    totals = jnp.sum(weights.astype(jnp.float32), axis=3)
    summed, totals = (summed, totals)
    attended = summed / jnp.transpose(totals, (0, 2, 1))[..., None]
    outgoing = (attended.reshape(rows, cols, heads_width) * gating).astype(jnp.bfloat16)
    result = after_tri.astype(jnp.float32) + jnp.dot(
        outgoing.reshape(-1, heads_width), att_out, preferred_element_type=jnp.float32
    ).reshape(rows, cols, channels)
    return result.astype(jnp.bfloat16)


MESH = pl.DeviceIdType.MESH
F32, BF16 = jnp.float32, jnp.bfloat16
NT = (((1,), (1,)), ((), ()))
TN = (((0,), (0,)), ((), ()))
NN = (((1,), (0,)), ((), ()))
MASKED = -3.0e38
VMEM_LIMIT = 60 * 1024 * 1024


def gate_of(values):
    return 0.5 * jnp.tanh(0.5 * values) + 0.5


def dot(a, b, dims=NN):
    return lax.dot_general(a, b, dims, preferred_element_type=F32)


def norm_rows(values):
    average = jnp.mean(values, axis=-1, keepdims=True)
    centred = values - average
    spread = jnp.mean(centred * centred, axis=-1, keepdims=True)
    return centred * lax.rsqrt(spread + EPSILON)


CHUNK = 4


def position(sizes):
    nr, nc, ns = sizes
    r = lax.axis_index("row")
    q = lax.axis_index("col") * ns + lax.axis_index("sub")

    def device(row, place):
        return {"row": row, "col": place // ns, "sub": lax.rem(place, ns)}

    return r, q, device


def peers_of(sizes):
    nr, nc, ns = sizes
    nq = nc * ns
    deep = nr // 2
    r, q, device = position(sizes)
    half, z = r // deep, lax.rem(r, deep)
    found = []
    for e in range(2):
        for d in range(deep):
            for o in range(nq):
                if e or d or o:
                    level, place = lax.rem(z + d, deep), lax.rem(q + o, nq)
                    row = lax.rem(half + e, 2) * deep + level
                    found.append((level * nq + place, row * nq + place, device(row, place), e == 0))
    return found


def columns_of(ids):
    spread = jnp.broadcast_to(ids.astype(F32), (128, ids.shape[1]))
    return spread.T.astype(jnp.int32)


def meet(devices):
    barrier = pltpu.get_barrier_semaphore()
    for where in devices:
        pl.semaphore_signal(barrier, inc=1, device_id=where, device_id_type=MESH)
    pl.semaphore_wait(barrier, len(devices))


def send(src, dst, send_sem, recv_sem, where):
    copy = pltpu.make_async_remote_copy(
        src_ref=src, dst_ref=dst, send_sem=send_sem, recv_sem=recv_sem,
        device_id=where, device_id_type=MESH,
    )
    copy.start()
    return copy


def project_kernel(
    sizes, chain_ids, residue_mask, chain_row, live_row, chain_vec, weight, pair_ref,
    rows_ref, left_ref, right_ref, left, right, chain_cols,
    in_send, in_recv, in_own, left_send, left_recv, right_send, right_recv, out_own,
):
    nr, nc, ns = sizes
    nq = nc * ns
    r, q, device = position(sizes)
    me = r * nq + q
    mine_in_half = lax.rem(r, nr // 2) * nq + q
    groups, own, wide, length = left.shape
    cols = length // nq
    chunks = own // CHUNK
    half = weight.shape[0] // 2
    side = half // 2
    peers = peers_of(sizes)
    meet([peer[2] for peer in peers])
    arriving = []
    for n in range(chunks):
        some = pl.ds(n * CHUNK, CHUNK)
        here = pl.ds(q * cols, cols)
        now = []
        for d in range(1, nq):
            p = lax.rem(q + d, nq)
            now.append(send(
                pair_ref.at[pl.ds(p * own + n * CHUNK, CHUNK)], rows_ref.at[some, here, :],
                in_send.at[n, d - 1], in_recv.at[n, d - 1], device(r, p),
            ))
        mine = pltpu.make_async_copy(
            pair_ref.at[pl.ds(q * own + n * CHUNK, CHUNK)], rows_ref.at[some, here, :], in_own.at[n]
        )
        mine.start()
        arriving.append((now, mine))
    chain_cols[...] = columns_of(chain_row[...])
    live_cols = live_row[...].astype(F32)
    leaving = []
    for n in range(chunks):
        now, mine = arriving[n]
        mine.wait()
        for copy in now:
            copy.wait_recv()

        @pl.loop(n * CHUNK, (n + 1) * CHUNK)
        def _(i):
            at = me * own + i
            same = jnp.where(chain_cols[...] == chain_ids[at], chain_vec[...], 0.0)
            normed = norm_rows(rows_ref[i].astype(F32) + same).astype(BF16)
            projected = dot(weight[...], normed, NT)
            mask = live_cols * residue_mask[at].astype(F32)
            both = (gate_of(projected[half:]) * projected[:half] * mask).astype(BF16)
            left[:, i] = both[:side].reshape(groups, wide, length)
            right[:, i] = both[side:].reshape(groups, wide, length)

        some = pl.ds(n * CHUNK, CHUNK)
        near = 0
        for d, (p, _, where, same_half) in enumerate(peers):
            leaving.append(send(
                right.at[p, some], right_ref.at[me, some], right_send.at[n, d], right_recv.at[n, d], where
            ))
            if same_half:
                leaving.append(send(
                    left.at[p, some], left_ref.at[mine_in_half, some],
                    left_send.at[n, near], left_recv.at[n, near], where,
                ))
                near += 1
        for k, (a, b) in enumerate((
            (left.at[mine_in_half, some], left_ref.at[mine_in_half, some]),
            (right.at[mine_in_half, some], right_ref.at[me, some]),
        )):
            mine = pltpu.make_async_copy(a, b, out_own.at[n, k])
            mine.start()
            leaving.append(mine)
    for now, _ in arriving:
        for copy in now:
            copy.wait_send()
    for copy in leaving:
        copy.wait()


def product_kernel(count, left_ref, right_ref, out_ref, *scratch):
    lanes = left_ref.shape[1] // 128
    left, right, made = scratch[:lanes], scratch[lanes : 2 * lanes], scratch[2 * lanes :]
    step = left_ref.shape[1]
    for source, flat in ((left_ref, left), (right_ref, right)):

        @pl.loop(0, source.shape[0] // step)
        def _(s):
            at = pl.ds(pl.multiple_of(s * step, step), step)
            for t in range(lanes):
                flat[t][at, :] = source[at, t * 128 : (t + 1) * 128].astype(F32)

    def channel(flat, c):
        at = pl.ds(c, flat[0].shape[0] // count, stride=count)
        return jnp.concatenate([part[at, :].astype(BF16) for part in flat], axis=1)

    for c in range(count):
        product = dot(channel(left, c), channel(right, c), NT)
        for t in range(lanes):
            made[t][pl.ds(c, product.shape[0], stride=count), :] = product[:, t * 128 : (t + 1) * 128]

    @pl.loop(0, out_ref.shape[0] // step)
    def _(s):
        at = pl.ds(pl.multiple_of(s * step, step), step)
        for t in range(lanes):
            out_ref[at, t * 128 : (t + 1) * 128] = made[t][at, :].astype(BF16)


def update_kernel(
    sizes, chain_ids, pair_ref, prod_ref, chain_row, live_row, chain_vec, tri_gate, tri_out, att_bias,
    after_ref, second_ref, gathered, landed, bias_ref, bias_out, chain_cols,
    in_send, in_recv, in_own, row_send, row_recv, col_send, col_recv, sub_send, sub_recv, own_sem,
):
    nr, nc, ns = sizes
    nq = nc * ns
    r, q, device = position(sizes)
    c, u = lax.axis_index("col"), lax.axis_index("sub")
    me = r * nq + q
    mine_in_half = lax.rem(r, nr // 2) * nq + q
    groups, tall, length = landed.shape
    own = pair_ref.shape[0]
    per = tall // own
    chunks = own // CHUNK
    near = [peer for peer in peers_of(sizes) if peer[3]]
    meet([peer[2] for peer in peers_of(sizes)])
    arriving = []
    for n in range(chunks):
        some = pl.ds(n * CHUNK * per, CHUNK * per)
        now = [
            send(prod_ref.at[p, some], landed.at[mine_in_half, some], in_send.at[n, d], in_recv.at[n, d], where)
            for d, (p, _, where, _) in enumerate(near)
        ]
        mine = pltpu.make_async_copy(
            prod_ref.at[mine_in_half, some], landed.at[mine_in_half, some], in_own.at[n]
        )
        mine.start()
        arriving.append((now, mine))
    chain_cols[...] = columns_of(chain_row[...])
    live_cols = live_row[...].astype(F32)
    for n in range(chunks):
        now, mine = arriving[n]
        mine.wait()
        for copy in now:
            copy.wait_recv()

        @pl.loop(n * CHUNK, (n + 1) * CHUNK)
        def _(i):
            at = pl.ds(pl.multiple_of(i * per, per), per)
            product = landed[:, at, :].astype(F32).reshape(groups * per, length)
            same = jnp.where(chain_cols[...] == chain_ids[me * own + i], chain_vec[...], 0.0)
            start = pair_ref[i].astype(F32) + same
            normed = norm_rows(start).astype(BF16)
            gating = gate_of(dot(normed, tri_gate[...]))
            average = jnp.mean(product, axis=0, keepdims=True)
            centred = product - average
            spread = jnp.mean(centred * centred, axis=0, keepdims=True)
            product_normed = (centred * lax.rsqrt(spread + EPSILON)).astype(BF16)
            after = (start + gating * dot(product_normed, tri_out[...], TN)).astype(BF16)
            second = norm_rows(after.astype(F32)).astype(BF16)
            after_ref[i] = after
            second_ref[i] = second
            bias = dot(att_bias[...], second, NT)
            bias = jnp.where(live_cols > 0.0, bias, MASKED)
            for h in range(HEADS):
                bias_ref[pl.ds(h * own + i, 1), :] = bias[h : h + 1, :]

    bias_out[...] = bias_ref[...].astype(BF16)
    mine = pltpu.make_async_copy(bias_out, gathered.at[q, r], own_sem)
    mine.start()
    hops = []
    for d in range(1, nr):
        hops.append(send(
            bias_out, gathered.at[q, r], row_send.at[d - 1], row_recv.at[d - 1],
            device(lax.rem(r + d, nr), q),
        ))
    mine.wait()
    for copy in hops:
        copy.wait_recv()
    across = []
    for d in range(1, nc):
        across.append(send(
            gathered.at[q], gathered.at[q], col_send.at[d - 1], col_recv.at[d - 1],
            device(r, lax.rem(c + d, nc) * ns + u),
        ))
    last = []

    def pass_on(e):
        source = lax.rem(c + nc - e, nc) * ns + u
        for d in range(1, ns):
            last.append(send(
                gathered.at[source], gathered.at[source], sub_send.at[e, d - 1], sub_recv.at[e, d - 1],
                device(r, c * ns + lax.rem(u + d, ns)),
            ))

    pass_on(0)
    for e, copy in enumerate(across):
        copy.wait_recv()
        pass_on(e + 1)
    for copy in last:
        copy.wait()
    for copy in hops + across:
        copy.wait_send()
    for now, _ in arriving:
        for copy in now:
            copy.wait_send()


def attend_kernel(
    sizes, second_ref, after_ref, bias_ref, att_query, att_kv, att_out,
    out_ref, made, out_send, out_recv, out_own,
):
    nr, nc, ns = sizes
    nq = nc * ns
    r, q, device = position(sizes)
    own, length, width = made.shape
    cols = length // nq
    others = [lax.rem(q + d, nq) for d in range(1, nq)]
    meet([device(r, p) for p in others])
    head = lax.broadcasted_iota(jnp.int32, (length, width), 1) // HEAD_DIM
    leaving = []
    for n in range(own // CHUNK):

        @pl.loop(n * CHUNK, (n + 1) * CHUNK)
        def _(i):
            second = second_ref[i]
            query_gate = dot(second, att_query[...])
            query = (query_gate[:, :width] * HEAD_DIM ** (-0.5)).astype(BF16)
            gating = gate_of(query_gate[:, width:])
            keyval = dot(second, att_kv[...]).astype(BF16)
            key, value = keyval[:, :width], keyval[:, width:]
            summed = None
            for h in range(HEADS):
                mine = (head == h).astype(BF16)
                scores = dot(query * mine, key, NT) + bias_ref[h]
                weights = jnp.exp(scores).astype(BF16)
                part = dot(weights, jnp.concatenate([value * mine, mine], axis=1))
                summed = part if summed is None else summed + part
            attended = summed[:, :width] / summed[:, width:]
            outgoing = (attended * gating).astype(BF16)
            result = after_ref[i].astype(F32) + dot(outgoing, att_out[...])
            made[i] = result.astype(BF16)

        some = pl.ds(n * CHUNK, CHUNK)
        to = pl.ds(q * own + n * CHUNK, CHUNK)
        for d, p in enumerate(others):
            leaving.append(send(
                made.at[some, pl.ds(p * cols, cols), :], out_ref.at[to],
                out_send.at[n, d], out_recv.at[n, d], device(r, p),
            ))
        mine = pltpu.make_async_copy(made.at[some, pl.ds(q * cols, cols), :], out_ref.at[to], out_own.at[n])
        mine.start()
        leaving.append(mine)
    for copy in leaving:
        copy.wait()


def by_rows(
    sizes,
    pair,
    chain_ids,
    residue_mask,
    chain_vec,
    tri_in,
    tri_gate,
    tri_out,
    att_query,
    att_kv,
    att_bias,
    att_out,
):
    nr, nc, ns = sizes
    nq = nc * ns
    groups = nr * nq
    rows, cols, channels = pair.shape
    own = rows // nq
    length = cols * nq
    near = groups // 2
    per = channels // near
    chain_row, live_row, chain_one = chain_ids[None, :], residue_mask[None, :], chain_vec[None, :]
    order = [tri_in[:, n * channels : (n + 1) * channels] for n in (0, 2, 1, 3)]
    weight = jnp.concatenate(order, axis=1).T
    bias_weight = jnp.pad(att_bias.T, ((0, 8 - HEADS), (0, 0)))

    chunks = own // CHUNK
    smem = pl.BlockSpec(memory_space=pltpu.SMEM)
    vmem = pl.BlockSpec(memory_space=pltpu.VMEM)
    anywhere = pl.BlockSpec(memory_space=pl.ANY)
    dma = pltpu.SemaphoreType.DMA
    row_shape = jax.ShapeDtypeStruct((own, length, channels), BF16)

    def params(n):
        return pltpu.CompilerParams(collective_id=n, has_side_effects=True, vmem_limit_bytes=VMEM_LIMIT)

    side_shape = (near, own, per, length)
    pair_rows, left, right = pl.pallas_call(
        functools.partial(project_kernel, sizes),
        in_specs=[smem, smem, vmem, vmem, vmem, vmem, anywhere],
        out_specs=[vmem, anywhere, anywhere],
        out_shape=[
            row_shape,
            jax.ShapeDtypeStruct(side_shape, BF16),
            jax.ShapeDtypeStruct((groups, own, per, length), BF16),
        ],
        scratch_shapes=[
            pltpu.VMEM(side_shape, BF16), pltpu.VMEM(side_shape, BF16), pltpu.VMEM((length, channels), jnp.int32),
            dma((chunks, nq - 1)), dma((chunks, nq - 1)), dma((chunks,)),
            dma((chunks, near - 1)), dma((chunks, near - 1)),
            dma((chunks, groups - 1)), dma((chunks, groups - 1)), dma((chunks, 2)),
        ],
        compiler_params=params(1),
        name="project",
    )(chain_ids, residue_mask, chain_row, live_row, chain_one, weight, pair)
    lanes = length // 128
    tall_left, tall_right = near * own * per, length * per
    product = pl.pallas_call(
        functools.partial(product_kernel, per),
        out_shape=jax.ShapeDtypeStruct((tall_left, length), BF16),
        in_specs=[vmem, vmem],
        out_specs=vmem,
        scratch_shapes=[pltpu.VMEM((tall_left, 128), F32)] * lanes
        + [pltpu.VMEM((tall_right, 128), F32)] * lanes
        + [pltpu.VMEM((tall_left, 128), F32)] * lanes,
        compiler_params=pltpu.CompilerParams(vmem_limit_bytes=VMEM_LIMIT),
        name="product",
    )(left.reshape(tall_left, length), right.reshape(tall_right, length))
    product = product.reshape(near, own * per, length)
    tall = HEADS * own
    after, second, bias_all = pl.pallas_call(
        functools.partial(update_kernel, sizes),
        in_specs=[smem, vmem, anywhere, vmem, vmem, vmem, vmem, vmem, vmem],
        out_specs=[vmem, vmem, vmem],
        out_shape=[row_shape, row_shape, jax.ShapeDtypeStruct((nq, nr, tall, length), BF16)],
        scratch_shapes=[
            pltpu.VMEM(product.shape, BF16), pltpu.VMEM((tall, length), F32), pltpu.VMEM((tall, length), BF16),
            pltpu.VMEM((length, channels), jnp.int32),
            dma((chunks, near - 1)), dma((chunks, near - 1)), dma((chunks,)),
            dma((max(nr - 1, 1),)), dma((max(nr - 1, 1),)),
            dma((max(nc - 1, 1),)), dma((max(nc - 1, 1),)),
            dma((nc, max(ns - 1, 1))), dma((nc, max(ns - 1, 1))), dma,
        ],
        compiler_params=params(2),
        name="update",
    )(chain_ids, pair_rows, product, chain_row, live_row, chain_one, tri_gate, tri_out, bias_weight)
    bias_all = jnp.transpose(bias_all.reshape(nq, nr, HEADS, own, length), (2, 1, 0, 3, 4))
    bias_all = bias_all.reshape(HEADS, length, length).astype(F32)
    return pl.pallas_call(
        functools.partial(attend_kernel, sizes),
        in_specs=[vmem] * 6,
        out_specs=anywhere,
        out_shape=jax.ShapeDtypeStruct((rows, cols, channels), BF16),
        scratch_shapes=[
            pltpu.VMEM(row_shape.shape, BF16),
            dma((chunks, nq - 1)), dma((chunks, nq - 1)), dma((chunks,)),
        ],
        compiler_params=params(3),
        name="attend",
    )(second, after, bias_all, att_query, att_kv, att_out)


def device_program(sizes, pair, *rest):
    rows, cols, channels = pair.shape
    nr, nc, ns = sizes
    nq = nc * ns
    length = cols * nq
    fits = (
        rows % (2 * nq) == 0
        and (rows // nq) % 8 == 0
        and cols % 16 == 0
        and channels == 128
        and nr % 2 == 0
        and channels == 8 * nr * nq
        and length % 128 == 0
        and length == rows * nr
    )
    if fits:
        return by_rows(sizes, pair, *rest)
    return on_device(pair, *rest)


def solution(mesh):
    sizes = tuple(mesh.shape[name] for name in ("row", "col", "sub"))
    return jax.shard_map(
        functools.partial(device_program, sizes),
        mesh=mesh,
        in_specs=(
            P(("grp", "row"), ("col", "sub"), None),
            P("grp"),
            P("grp"),
            P(),
            P(),
            P(),
            P(),
            P(),
            P(),
            P(),
            P(),
        ),
        out_specs=P(("grp", "row"), ("col", "sub"), None),
        check_vma=False,
    )
```

```python
import functools

import jax
import jax.numpy as jnp
from jax import lax
from jax.experimental import pallas as pl
from jax.experimental.pallas import tpu as pltpu
from jax.sharding import PartitionSpec as P

HEADS = 4
HEAD_DIM = 32


EPSILON = 1e-05


def layer_norm(values):
    average = jnp.mean(values, axis=-1, keepdims=True)
    centred = values - average
    spread = jnp.mean(centred * centred, axis=-1, keepdims=True)
    return centred * lax.rsqrt(spread + EPSILON)


def on_device(
    pair,
    chain_ids,
    residue_mask,
    chain_vec,
    tri_in,
    tri_gate,
    tri_out,
    att_query,
    att_kv,
    att_bias,
    att_out,
):
    rows, cols, channels = pair.shape
    heads_width = HEADS * HEAD_DIM
    row_start = lax.axis_index("row") * rows
    col_block = lax.axis_index(("col", "sub"))
    col_start = col_block * cols
    living = residue_mask.astype(jnp.float32)
    row_live = lax.dynamic_slice_in_dim(living, row_start, rows)
    col_live = lax.dynamic_slice_in_dim(living, col_start, cols)
    row_chain = lax.dynamic_slice_in_dim(chain_ids, row_start, rows)
    col_chain = lax.dynamic_slice_in_dim(chain_ids, col_start, cols)
    same_chain = (row_chain[:, None] == col_chain[None, :]).astype(jnp.float32)
    pair_mask = row_live[:, None] * col_live[None, :]
    start_pair = pair.astype(jnp.float32) + same_chain[:, :, None] * chain_vec
    normed = layer_norm(start_pair).astype(jnp.bfloat16)
    flat_rows = normed.reshape(rows * cols, channels)
    projected = jnp.dot(flat_rows, tri_in, preferred_element_type=jnp.float32).reshape(
        rows, cols, 4 * channels
    )
    left_side = (
        jax.nn.sigmoid(projected[..., channels : 2 * channels])
        * projected[..., :channels]
        * pair_mask[..., None]
    )
    right_side = (
        jax.nn.sigmoid(projected[..., 3 * channels :])
        * projected[..., 2 * channels : 3 * channels]
        * pair_mask[..., None]
    )
    stacked = jnp.transpose(jnp.stack([left_side, right_side]).astype(jnp.bfloat16), (0, 3, 1, 2))
    regrouped = lax.all_to_all(
        lax.all_to_all(stacked, "row", split_axis=1, concat_axis=2, tiled=True),
        ("col", "sub"),
        split_axis=2,
        concat_axis=3,
        tiled=True,
    )
    left_part = regrouped[0]
    right_part = regrouped[1]
    product = jnp.einsum(
        "cjk,cik->cji",
        right_part,
        lax.all_gather(left_part, ("col", "sub"), axis=1, tiled=True),
        preferred_element_type=jnp.float32,
    ).astype(jnp.bfloat16)
    returned = lax.all_to_all(product, "row", split_axis=2, concat_axis=0, tiled=True)
    product_pairs = jnp.transpose(returned, (2, 1, 0)).astype(jnp.float32)
    tri_gating = jax.nn.sigmoid(
        jnp.dot(flat_rows, tri_gate, preferred_element_type=jnp.float32)
    ).reshape(rows, cols, channels)
    product_normed = layer_norm(product_pairs).astype(jnp.bfloat16)
    tri_update = tri_gating * jnp.dot(
        product_normed.reshape(-1, channels), tri_out, preferred_element_type=jnp.float32
    ).reshape(rows, cols, channels)
    after_tri = (start_pair + tri_update).astype(jnp.bfloat16)
    second = layer_norm(after_tri.astype(jnp.float32)).astype(jnp.bfloat16)
    flat_second = second.reshape(-1, channels)
    query_gate = jnp.dot(flat_second, att_query, preferred_element_type=jnp.float32).reshape(
        rows, cols, 2 * heads_width
    )
    query = (
        (query_gate[..., :heads_width] * HEAD_DIM ** (-0.5))
        .astype(jnp.bfloat16)
        .reshape(rows, cols, HEADS, HEAD_DIM)
    )
    gating = jax.nn.sigmoid(query_gate[..., heads_width:])
    local_bias = (
        jnp.dot(flat_second, att_bias, preferred_element_type=jnp.float32)
        .astype(jnp.bfloat16)
        .reshape(rows, cols, HEADS)
    )
    local_bias = jnp.transpose(local_bias, (2, 0, 1))
    column_all = lax.all_gather(local_bias, "row", axis=1, tiled=True)
    bias_rows = lax.all_to_all(column_all, ("col", "sub"), split_axis=1, concat_axis=2, tiled=True)
    piece = lax.all_gather(second, ("col", "sub"), axis=1, tiled=True)
    width = piece.shape[1]
    keyval = (
        jnp.dot(piece.reshape(-1, channels), att_kv, preferred_element_type=jnp.float32)
        .astype(jnp.bfloat16)
        .reshape(rows, width, 2 * heads_width)
    )
    width = keyval.shape[1]
    key_heads = keyval[..., :heads_width].reshape(rows, width, HEADS, HEAD_DIM)
    value_heads = keyval[..., heads_width:].reshape(rows, width, HEADS, HEAD_DIM)
    scores = jnp.einsum("ijhd,ikhd->ihjk", query, key_heads, preferred_element_type=jnp.float32)
    scores = scores + bias_rows.astype(jnp.float32)[None]
    weights = (jnp.exp(scores) * living).astype(jnp.bfloat16)
    summed = jnp.einsum("ihjk,ikhd->ijhd", weights, value_heads, preferred_element_type=jnp.float32)
    totals = jnp.sum(weights.astype(jnp.float32), axis=3)
    summed, totals = (summed, totals)
    attended = summed / jnp.transpose(totals, (0, 2, 1))[..., None]
    outgoing = (attended.reshape(rows, cols, heads_width) * gating).astype(jnp.bfloat16)
    result = after_tri.astype(jnp.float32) + jnp.dot(
        outgoing.reshape(-1, heads_width), att_out, preferred_element_type=jnp.float32
    ).reshape(rows, cols, channels)
    return result.astype(jnp.bfloat16)


MESH = pl.DeviceIdType.MESH
F32, BF16 = jnp.float32, jnp.bfloat16
NT = (((1,), (1,)), ((), ()))
TN = (((0,), (0,)), ((), ()))
NN = (((1,), (0,)), ((), ()))
MASKED = -3.0e38
VMEM_LIMIT = 60 * 1024 * 1024


def gate_of(values):
    return 0.5 * jnp.tanh(0.5 * values) + 0.5


def dot(a, b, dims=NN):
    return lax.dot_general(a, b, dims, preferred_element_type=F32)


def norm_rows(values):
    average = jnp.mean(values, axis=-1, keepdims=True)
    centred = values - average
    spread = jnp.mean(centred * centred, axis=-1, keepdims=True)
    return centred * lax.rsqrt(spread + EPSILON)


CHUNK = 4


def position(sizes):
    nr, nc, ns = sizes
    r = lax.axis_index("row")
    q = lax.axis_index("col") * ns + lax.axis_index("sub")

    def device(row, place):
        return {"row": row, "col": place // ns, "sub": lax.rem(place, ns)}

    return r, q, device


def peers_of(sizes):
    nr, nc, ns = sizes
    nq = nc * ns
    deep = nr // 2
    r, q, device = position(sizes)
    half, z = r // deep, lax.rem(r, deep)
    found = []
    for e in range(2):
        for d in range(deep):
            for o in range(nq):
                if e or d or o:
                    level, place = lax.rem(z + d, deep), lax.rem(q + o, nq)
                    row = lax.rem(half + e, 2) * deep + level
                    found.append((level * nq + place, row * nq + place, device(row, place), e == 0))
    return found


def columns_of(ids):
    spread = jnp.broadcast_to(ids.astype(F32), (128, ids.shape[1]))
    return spread.T.astype(jnp.int32)


def meet(devices):
    barrier = pltpu.get_barrier_semaphore()
    for where in devices:
        pl.semaphore_signal(barrier, inc=1, device_id=where, device_id_type=MESH)
    pl.semaphore_wait(barrier, len(devices))


def send(src, dst, send_sem, recv_sem, where):
    copy = pltpu.make_async_remote_copy(
        src_ref=src, dst_ref=dst, send_sem=send_sem, recv_sem=recv_sem,
        device_id=where, device_id_type=MESH,
    )
    copy.start()
    return copy


def project_kernel(
    sizes, chain_ids, residue_mask, chain_row, live_row, chain_vec, weight, pair_ref,
    rows_ref, left_ref, right_ref, left, right, chain_cols,
    in_send, in_recv, in_own, left_send, left_recv, right_send, right_recv, out_own,
):
    nr, nc, ns = sizes
    nq = nc * ns
    r, q, device = position(sizes)
    me = r * nq + q
    mine_in_half = lax.rem(r, nr // 2) * nq + q
    groups, own, wide, length = left.shape
    cols = length // nq
    chunks = own // CHUNK
    half = weight.shape[0] // 2
    side = half // 2
    peers = peers_of(sizes)
    meet([peer[2] for peer in peers])
    arriving = []
    for n in range(chunks):
        some = pl.ds(n * CHUNK, CHUNK)
        here = pl.ds(q * cols, cols)
        now = []
        for d in range(1, nq):
            p = lax.rem(q + d, nq)
            now.append(send(
                pair_ref.at[pl.ds(p * own + n * CHUNK, CHUNK)], rows_ref.at[some, here, :],
                in_send.at[n, d - 1], in_recv.at[n, d - 1], device(r, p),
            ))
        mine = pltpu.make_async_copy(
            pair_ref.at[pl.ds(q * own + n * CHUNK, CHUNK)], rows_ref.at[some, here, :], in_own.at[n]
        )
        mine.start()
        arriving.append((now, mine))
    chain_cols[...] = columns_of(chain_row[...])
    live_cols = live_row[...].astype(F32)
    leaving = []
    for n in range(chunks):
        now, mine = arriving[n]
        mine.wait()
        for copy in now:
            copy.wait_recv()

        @pl.loop(n * CHUNK, (n + 1) * CHUNK)
        def _(i):
            at = me * own + i
            same = jnp.where(chain_cols[...] == chain_ids[at], chain_vec[...], 0.0)
            normed = norm_rows(rows_ref[i].astype(F32) + same).astype(BF16)
            projected = dot(weight[...], normed, NT)
            mask = live_cols * residue_mask[at].astype(F32)
            both = (gate_of(projected[half:]) * projected[:half] * mask).astype(BF16)
            left[:, i] = both[:side].reshape(groups, wide, length)
            right[:, i] = both[side:].reshape(groups, wide, length)

        some = pl.ds(n * CHUNK, CHUNK)
        near = 0
        for d, (p, _, where, same_half) in enumerate(peers):
            leaving.append(send(
                right.at[p, some], right_ref.at[me, some], right_send.at[n, d], right_recv.at[n, d], where
            ))
            if same_half:
                leaving.append(send(
                    left.at[p, some], left_ref.at[mine_in_half, some],
                    left_send.at[n, near], left_recv.at[n, near], where,
                ))
                near += 1
        for k, (a, b) in enumerate((
            (left.at[mine_in_half, some], left_ref.at[mine_in_half, some]),
            (right.at[mine_in_half, some], right_ref.at[me, some]),
        )):
            mine = pltpu.make_async_copy(a, b, out_own.at[n, k])
            mine.start()
            leaving.append(mine)
    for now, _ in arriving:
        for copy in now:
            copy.wait_send()
    for copy in leaving:
        copy.wait()


def multiply(count, left_ref, right_ref, out_ref, scratch):
    lanes = left_ref.shape[1] // 128
    left, right, made = scratch[:lanes], scratch[lanes : 2 * lanes], scratch[2 * lanes :]
    step = left_ref.shape[1]
    for source, flat in ((left_ref, left), (right_ref, right)):

        @pl.loop(0, source.shape[0] // step)
        def _(s):
            at = pl.ds(pl.multiple_of(s * step, step), step)
            for t in range(lanes):
                flat[t][at, :] = source[at, t * 128 : (t + 1) * 128].astype(F32)

    def channel(flat, c):
        at = pl.ds(c, flat[0].shape[0] // count, stride=count)
        return jnp.concatenate([part[at, :].astype(BF16) for part in flat], axis=1)

    for c in range(count):
        product = dot(channel(left, c), channel(right, c), NT)
        for t in range(lanes):
            made[t][pl.ds(c, product.shape[0], stride=count), :] = product[:, t * 128 : (t + 1) * 128]

    tall = out_ref.shape[1]

    @pl.loop(0, out_ref.shape[0])
    def _(g):
        at = pl.ds(pl.multiple_of(g * tall, tall), tall)
        for t in range(lanes):
            out_ref[g, :, t * 128 : (t + 1) * 128] = made[t][at, :].astype(BF16)


def finish_kernel(
    sizes, chain_ids, left_ref, right_ref, pair_ref, chain_row, live_row, chain_vec, tri_gate, tri_out, att_bias,
    att_query, att_kv, att_out,
    out_ref, prod_ref, landed, bias_ref, bias_out, chain_cols, gathered, bias_full,
    after_ref, second_ref, query_ref, key_ref, value_ref, made,
    in_send, in_recv, in_own, row_send, row_recv, col_send, col_recv, sub_send, sub_recv, own_sem,
    out_send, out_recv, out_own, *flat,
):
    nr, nc, ns = sizes
    nq = nc * ns
    r, q, device = position(sizes)
    c, u = lax.axis_index("col"), lax.axis_index("sub")
    me = r * nq + q
    mine_in_half = lax.rem(r, nr // 2) * nq + q
    groups, tall, length = landed.shape
    own = pair_ref.shape[0]
    per = tall // own
    chunks = own // CHUNK
    width = HEADS * HEAD_DIM
    cols = length // nq
    near = [peer for peer in peers_of(sizes) if peer[3]]
    others = [lax.rem(q + d, nq) for d in range(1, nq)]
    meet([peer[2] for peer in peers_of(sizes)])
    multiply(per, left_ref, right_ref, prod_ref, flat)
    arriving = []
    for n in range(chunks):
        some = pl.ds(n * CHUNK * per, CHUNK * per)
        now = [
            send(prod_ref.at[p, some], landed.at[mine_in_half, some], in_send.at[n, d], in_recv.at[n, d], where)
            for d, (p, _, where, _) in enumerate(near)
        ]
        mine = pltpu.make_async_copy(
            prod_ref.at[mine_in_half, some], landed.at[mine_in_half, some], in_own.at[n]
        )
        mine.start()
        arriving.append((now, mine))
    chain_cols[...] = columns_of(chain_row[...])
    live_cols = live_row[...].astype(F32)
    for n in range(chunks):
        now, mine = arriving[n]
        mine.wait()
        for copy in now:
            copy.wait_recv()

        @pl.loop(n * CHUNK, (n + 1) * CHUNK)
        def _(i):
            at = pl.ds(pl.multiple_of(i * per, per), per)
            product = landed[:, at, :].astype(F32).reshape(groups * per, length)
            same = jnp.where(chain_cols[...] == chain_ids[me * own + i], chain_vec[...], 0.0)
            start = pair_ref[i].astype(F32) + same
            normed = norm_rows(start).astype(BF16)
            gating = gate_of(dot(normed, tri_gate[...]))
            average = jnp.mean(product, axis=0, keepdims=True)
            centred = product - average
            spread = jnp.mean(centred * centred, axis=0, keepdims=True)
            product_normed = (centred * lax.rsqrt(spread + EPSILON)).astype(BF16)
            after = (start + gating * dot(product_normed, tri_out[...], TN)).astype(BF16)
            second = norm_rows(after.astype(F32)).astype(BF16)
            after_ref[i] = after
            second_ref[i] = second
            bias = dot(att_bias[...], second, NT)
            bias = jnp.where(live_cols > 0.0, bias, MASKED)
            for h in range(HEADS):
                bias_ref[pl.ds(h * own + i, 1), :] = bias[h : h + 1, :]

    bias_out[...] = bias_ref[...].astype(BF16)
    mine = pltpu.make_async_copy(bias_out, gathered.at[q, r], own_sem)
    mine.start()
    hops = []
    for d in range(1, nr):
        hops.append(send(
            bias_out, gathered.at[q, r], row_send.at[d - 1], row_recv.at[d - 1],
            device(lax.rem(r + d, nr), q),
        ))

    def prepare(first, past):
        @pl.loop(first, past)
        def _(i):
            second = second_ref[i]
            query = dot(second, att_query[:, :width])
            query_ref[i] = (query * HEAD_DIM ** (-0.5)).astype(BF16)
            keyval = dot(second, att_kv[...]).astype(BF16)
            key_ref[i] = keyval[:, :width]
            value_ref[i] = keyval[:, width:]

    prepare(0, own // 2)
    mine.wait()
    for copy in hops:
        copy.wait_recv()
    across = []
    for d in range(1, nc):
        across.append(send(
            gathered.at[q], gathered.at[q], col_send.at[d - 1], col_recv.at[d - 1],
            device(r, lax.rem(c + d, nc) * ns + u),
        ))
    last = []

    def pass_on(e):
        source = lax.rem(c + nc - e, nc) * ns + u
        for d in range(1, ns):
            last.append(send(
                gathered.at[source], gathered.at[source], sub_send.at[e, d - 1], sub_recv.at[e, d - 1],
                device(r, c * ns + lax.rem(u + d, ns)),
            ))

    pass_on(0)
    prepare(own // 2, own)
    for e, copy in enumerate(across):
        copy.wait_recv()
        pass_on(e + 1)
    for copy in last:
        copy.wait()
    for copy in hops + across:
        copy.wait_send()
    for now, _ in arriving:
        for copy in now:
            copy.wait_send()
    for row in range(nr):
        for place in range(nq):
            block = gathered[place, row].astype(F32)
            for h in range(HEADS):
                bias_full[h, (row * nq + place) * own : (row * nq + place + 1) * own, :] = block[h * own : (h + 1) * own]
    head = lax.broadcasted_iota(jnp.int32, (length, width), 1) // HEAD_DIM
    leaving = []
    for n in range(own // CHUNK):

        @pl.loop(n * CHUNK, (n + 1) * CHUNK)
        def _(i):
            second = second_ref[i]
            gating = gate_of(dot(second, att_query[:, width:]))
            query, key, value = query_ref[i], key_ref[i], value_ref[i]
            summed = None
            for h in range(HEADS):
                mine = (head == h).astype(BF16)
                scores = dot(query * mine, key, NT) + bias_full[h]
                weights = jnp.exp(scores).astype(BF16)
                part = dot(weights, jnp.concatenate([value * mine, mine], axis=1))
                summed = part if summed is None else summed + part
            attended = summed[:, :width] / summed[:, width:]
            outgoing = (attended * gating).astype(BF16)
            result = after_ref[i].astype(F32) + dot(outgoing, att_out[...])
            made[i] = result.astype(BF16)

        some = pl.ds(n * CHUNK, CHUNK)
        to = pl.ds(q * own + n * CHUNK, CHUNK)
        for d, p in enumerate(others):
            leaving.append(send(
                made.at[some, pl.ds(p * cols, cols), :], out_ref.at[to],
                out_send.at[n, d], out_recv.at[n, d], device(r, p),
            ))
        mine = pltpu.make_async_copy(made.at[some, pl.ds(q * cols, cols), :], out_ref.at[to], out_own.at[n])
        mine.start()
        leaving.append(mine)
    for copy in leaving:
        copy.wait()


def by_rows(
    sizes,
    pair,
    chain_ids,
    residue_mask,
    chain_vec,
    tri_in,
    tri_gate,
    tri_out,
    att_query,
    att_kv,
    att_bias,
    att_out,
):
    nr, nc, ns = sizes
    nq = nc * ns
    groups = nr * nq
    rows, cols, channels = pair.shape
    own = rows // nq
    length = cols * nq
    near = groups // 2
    per = channels // near
    chain_row, live_row, chain_one = chain_ids[None, :], residue_mask[None, :], chain_vec[None, :]
    order = [tri_in[:, n * channels : (n + 1) * channels] for n in (0, 2, 1, 3)]
    weight = jnp.concatenate(order, axis=1).T
    bias_weight = jnp.pad(att_bias.T, ((0, 8 - HEADS), (0, 0)))

    chunks = own // CHUNK
    smem = pl.BlockSpec(memory_space=pltpu.SMEM)
    vmem = pl.BlockSpec(memory_space=pltpu.VMEM)
    anywhere = pl.BlockSpec(memory_space=pl.ANY)
    dma = pltpu.SemaphoreType.DMA
    row_shape = jax.ShapeDtypeStruct((own, length, channels), BF16)

    def params(n):
        return pltpu.CompilerParams(collective_id=n, has_side_effects=True, vmem_limit_bytes=VMEM_LIMIT)

    side_shape = (near, own, per, length)
    pair_rows, left, right = pl.pallas_call(
        functools.partial(project_kernel, sizes),
        in_specs=[smem, smem, vmem, vmem, vmem, vmem, anywhere],
        out_specs=[vmem, anywhere, anywhere],
        out_shape=[
            row_shape,
            jax.ShapeDtypeStruct(side_shape, BF16),
            jax.ShapeDtypeStruct((groups, own, per, length), BF16),
        ],
        scratch_shapes=[
            pltpu.VMEM(side_shape, BF16), pltpu.VMEM(side_shape, BF16), pltpu.VMEM((length, channels), jnp.int32),
            dma((chunks, nq - 1)), dma((chunks, nq - 1)), dma((chunks,)),
            dma((chunks, near - 1)), dma((chunks, near - 1)),
            dma((chunks, groups - 1)), dma((chunks, groups - 1)), dma((chunks, 2)),
        ],
        compiler_params=params(1),
        name="project",
    )(chain_ids, residue_mask, chain_row, live_row, chain_one, weight, pair)
    lanes = length // 128
    tall_left, tall_right = near * own * per, length * per
    tall = HEADS * own
    rows_bf16 = pltpu.VMEM(row_shape.shape, BF16)
    return pl.pallas_call(
        functools.partial(finish_kernel, sizes),
        in_specs=[smem] + [vmem] * 12,
        out_specs=anywhere,
        out_shape=jax.ShapeDtypeStruct((rows, cols, channels), BF16),
        scratch_shapes=[
            pltpu.VMEM((near, own * per, length), BF16), pltpu.VMEM((near, own * per, length), BF16),
            pltpu.VMEM((tall, length), F32), pltpu.VMEM((tall, length), BF16),
            pltpu.VMEM((length, channels), jnp.int32),
            pltpu.VMEM((nq, nr, tall, length), BF16), pltpu.VMEM((HEADS, length, length), F32),
            rows_bf16, rows_bf16, rows_bf16, rows_bf16, rows_bf16, rows_bf16,
            dma((chunks, near - 1)), dma((chunks, near - 1)), dma((chunks,)),
            dma((max(nr - 1, 1),)), dma((max(nr - 1, 1),)),
            dma((max(nc - 1, 1),)), dma((max(nc - 1, 1),)),
            dma((nc, max(ns - 1, 1))), dma((nc, max(ns - 1, 1))), dma,
            dma((chunks, nq - 1)), dma((chunks, nq - 1)), dma((chunks,)),
        ]
        + [pltpu.VMEM((tall_left, 128), F32)] * lanes
        + [pltpu.VMEM((tall_right, 128), F32)] * lanes
        + [pltpu.VMEM((tall_left, 128), F32)] * lanes,
        compiler_params=params(2),
        name="finish",
    )(
        chain_ids, left.reshape(tall_left, length), right.reshape(tall_right, length), pair_rows,
        chain_row, live_row, chain_one, tri_gate, tri_out, bias_weight, att_query, att_kv, att_out,
    )


def device_program(sizes, pair, *rest):
    rows, cols, channels = pair.shape
    nr, nc, ns = sizes
    nq = nc * ns
    length = cols * nq
    fits = (
        rows % (2 * nq) == 0
        and (rows // nq) % 8 == 0
        and cols % 16 == 0
        and channels == 128
        and nr % 2 == 0
        and channels == 8 * nr * nq
        and length % 128 == 0
        and length == rows * nr
    )
    if fits:
        return by_rows(sizes, pair, *rest)
    return on_device(pair, *rest)


def solution(mesh):
    sizes = tuple(mesh.shape[name] for name in ("row", "col", "sub"))
    return jax.shard_map(
        functools.partial(device_program, sizes),
        mesh=mesh,
        in_specs=(
            P(("grp", "row"), ("col", "sub"), None),
            P("grp"),
            P("grp"),
            P(),
            P(),
            P(),
            P(),
            P(),
            P(),
            P(),
            P(),
        ),
        out_specs=P(("grp", "row"), ("col", "sub"), None),
        check_vma=False,
    )
```

```python
import functools

import jax
import jax.numpy as jnp
from jax import lax
from jax.experimental import pallas as pl
from jax.experimental.pallas import tpu as pltpu
from jax.sharding import PartitionSpec as P

HEADS = 4
HEAD_DIM = 32


EPSILON = 1e-05


def layer_norm(values):
    average = jnp.mean(values, axis=-1, keepdims=True)
    centred = values - average
    spread = jnp.mean(centred * centred, axis=-1, keepdims=True)
    return centred * lax.rsqrt(spread + EPSILON)


def on_device(
    pair,
    chain_ids,
    residue_mask,
    chain_vec,
    tri_in,
    tri_gate,
    tri_out,
    att_query,
    att_kv,
    att_bias,
    att_out,
):
    rows, cols, channels = pair.shape
    heads_width = HEADS * HEAD_DIM
    row_start = lax.axis_index("row") * rows
    col_block = lax.axis_index(("col", "sub"))
    col_start = col_block * cols
    living = residue_mask.astype(jnp.float32)
    row_live = lax.dynamic_slice_in_dim(living, row_start, rows)
    col_live = lax.dynamic_slice_in_dim(living, col_start, cols)
    row_chain = lax.dynamic_slice_in_dim(chain_ids, row_start, rows)
    col_chain = lax.dynamic_slice_in_dim(chain_ids, col_start, cols)
    same_chain = (row_chain[:, None] == col_chain[None, :]).astype(jnp.float32)
    pair_mask = row_live[:, None] * col_live[None, :]
    start_pair = pair.astype(jnp.float32) + same_chain[:, :, None] * chain_vec
    normed = layer_norm(start_pair).astype(jnp.bfloat16)
    flat_rows = normed.reshape(rows * cols, channels)
    projected = jnp.dot(flat_rows, tri_in, preferred_element_type=jnp.float32).reshape(
        rows, cols, 4 * channels
    )
    left_side = (
        jax.nn.sigmoid(projected[..., channels : 2 * channels])
        * projected[..., :channels]
        * pair_mask[..., None]
    )
    right_side = (
        jax.nn.sigmoid(projected[..., 3 * channels :])
        * projected[..., 2 * channels : 3 * channels]
        * pair_mask[..., None]
    )
    stacked = jnp.transpose(jnp.stack([left_side, right_side]).astype(jnp.bfloat16), (0, 3, 1, 2))
    regrouped = lax.all_to_all(
        lax.all_to_all(stacked, "row", split_axis=1, concat_axis=2, tiled=True),
        ("col", "sub"),
        split_axis=2,
        concat_axis=3,
        tiled=True,
    )
    left_part = regrouped[0]
    right_part = regrouped[1]
    product = jnp.einsum(
        "cjk,cik->cji",
        right_part,
        lax.all_gather(left_part, ("col", "sub"), axis=1, tiled=True),
        preferred_element_type=jnp.float32,
    ).astype(jnp.bfloat16)
    returned = lax.all_to_all(product, "row", split_axis=2, concat_axis=0, tiled=True)
    product_pairs = jnp.transpose(returned, (2, 1, 0)).astype(jnp.float32)
    tri_gating = jax.nn.sigmoid(
        jnp.dot(flat_rows, tri_gate, preferred_element_type=jnp.float32)
    ).reshape(rows, cols, channels)
    product_normed = layer_norm(product_pairs).astype(jnp.bfloat16)
    tri_update = tri_gating * jnp.dot(
        product_normed.reshape(-1, channels), tri_out, preferred_element_type=jnp.float32
    ).reshape(rows, cols, channels)
    after_tri = (start_pair + tri_update).astype(jnp.bfloat16)
    second = layer_norm(after_tri.astype(jnp.float32)).astype(jnp.bfloat16)
    flat_second = second.reshape(-1, channels)
    query_gate = jnp.dot(flat_second, att_query, preferred_element_type=jnp.float32).reshape(
        rows, cols, 2 * heads_width
    )
    query = (
        (query_gate[..., :heads_width] * HEAD_DIM ** (-0.5))
        .astype(jnp.bfloat16)
        .reshape(rows, cols, HEADS, HEAD_DIM)
    )
    gating = jax.nn.sigmoid(query_gate[..., heads_width:])
    local_bias = (
        jnp.dot(flat_second, att_bias, preferred_element_type=jnp.float32)
        .astype(jnp.bfloat16)
        .reshape(rows, cols, HEADS)
    )
    local_bias = jnp.transpose(local_bias, (2, 0, 1))
    column_all = lax.all_gather(local_bias, "row", axis=1, tiled=True)
    bias_rows = lax.all_to_all(column_all, ("col", "sub"), split_axis=1, concat_axis=2, tiled=True)
    piece = lax.all_gather(second, ("col", "sub"), axis=1, tiled=True)
    width = piece.shape[1]
    keyval = (
        jnp.dot(piece.reshape(-1, channels), att_kv, preferred_element_type=jnp.float32)
        .astype(jnp.bfloat16)
        .reshape(rows, width, 2 * heads_width)
    )
    width = keyval.shape[1]
    key_heads = keyval[..., :heads_width].reshape(rows, width, HEADS, HEAD_DIM)
    value_heads = keyval[..., heads_width:].reshape(rows, width, HEADS, HEAD_DIM)
    scores = jnp.einsum("ijhd,ikhd->ihjk", query, key_heads, preferred_element_type=jnp.float32)
    scores = scores + bias_rows.astype(jnp.float32)[None]
    weights = (jnp.exp(scores) * living).astype(jnp.bfloat16)
    summed = jnp.einsum("ihjk,ikhd->ijhd", weights, value_heads, preferred_element_type=jnp.float32)
    totals = jnp.sum(weights.astype(jnp.float32), axis=3)
    summed, totals = (summed, totals)
    attended = summed / jnp.transpose(totals, (0, 2, 1))[..., None]
    outgoing = (attended.reshape(rows, cols, heads_width) * gating).astype(jnp.bfloat16)
    result = after_tri.astype(jnp.float32) + jnp.dot(
        outgoing.reshape(-1, heads_width), att_out, preferred_element_type=jnp.float32
    ).reshape(rows, cols, channels)
    return result.astype(jnp.bfloat16)


MESH = pl.DeviceIdType.MESH
F32, BF16 = jnp.float32, jnp.bfloat16
NT = (((1,), (1,)), ((), ()))
TN = (((0,), (0,)), ((), ()))
NN = (((1,), (0,)), ((), ()))
MASKED = -3.0e38
VMEM_LIMIT = 60 * 1024 * 1024


def gate_of(values):
    return 0.5 * jnp.tanh(0.5 * values) + 0.5


def dot(a, b, dims=NN):
    return lax.dot_general(a, b, dims, preferred_element_type=F32)


def norm_rows(values):
    average = jnp.mean(values, axis=-1, keepdims=True)
    centred = values - average
    spread = jnp.mean(centred * centred, axis=-1, keepdims=True)
    return centred * lax.rsqrt(spread + EPSILON)


CHUNK = 4


def position(sizes):
    nr, nc, ns = sizes
    r = lax.axis_index("row")
    q = lax.axis_index("col") * ns + lax.axis_index("sub")

    def device(row, place):
        return {"row": row, "col": place // ns, "sub": lax.rem(place, ns)}

    return r, q, device


def peers_of(sizes):
    nr, nc, ns = sizes
    nq = nc * ns
    deep = nr // 2
    r, q, device = position(sizes)
    half, z = r // deep, lax.rem(r, deep)
    found = []
    for e in range(2):
        for d in range(deep):
            for o in range(nq):
                if e or d or o:
                    level, place = lax.rem(z + d, deep), lax.rem(q + o, nq)
                    row = lax.rem(half + e, 2) * deep + level
                    found.append((level * nq + place, row * nq + place, device(row, place), e == 0))
    return found


def columns_of(ids):
    spread = jnp.broadcast_to(ids.astype(F32)[None, :], (128, ids.shape[0]))
    return spread.T.astype(jnp.int32)


def meet(devices):
    barrier = pltpu.get_barrier_semaphore()
    for where in devices:
        pl.semaphore_signal(barrier, inc=1, device_id=where, device_id_type=MESH)
    pl.semaphore_wait(barrier, len(devices))


def send(src, dst, send_sem, recv_sem, where):
    copy = pltpu.make_async_remote_copy(
        src_ref=src, dst_ref=dst, send_sem=send_sem, recv_sem=recv_sem,
        device_id=where, device_id_type=MESH,
    )
    copy.start()
    return copy


def project_kernel(
    sizes, chain_ids, residue_mask, chain_row, live_row, chain_vec, weight, pair_ref,
    rows_ref, left_ref, right_ref, left, right, chain_cols,
    in_send, in_recv, in_own, left_send, left_recv, right_send, right_recv, out_own,
):
    nr, nc, ns = sizes
    nq = nc * ns
    r, q, device = position(sizes)
    me = r * nq + q
    mine_in_half = lax.rem(r, nr // 2) * nq + q
    groups, own, wide, length = left.shape
    cols = length // nq
    chunks = own // CHUNK
    half = weight.shape[0] // 2
    side = half // 2
    peers = peers_of(sizes)
    meet([peer[2] for peer in peers])
    arriving = []
    for n in range(chunks):
        some = pl.ds(n * CHUNK, CHUNK)
        here = pl.ds(q * cols, cols)
        now = []
        for d in range(1, nq):
            p = lax.rem(q + d, nq)
            now.append(send(
                pair_ref.at[pl.ds(p * own + n * CHUNK, CHUNK)], rows_ref.at[some, here, :],
                in_send.at[n, d - 1], in_recv.at[n, d - 1], device(r, p),
            ))
        mine = pltpu.make_async_copy(
            pair_ref.at[pl.ds(q * own + n * CHUNK, CHUNK)], rows_ref.at[some, here, :], in_own.at[n]
        )
        mine.start()
        arriving.append((now, mine))
    chain_cols[...] = columns_of(chain_row[...])
    live_cols = live_row[...].astype(F32)[None, :]
    leaving = []
    for n in range(chunks):
        now, mine = arriving[n]
        mine.wait()
        for copy in now:
            copy.wait_recv()

        @pl.loop(n * CHUNK, (n + 1) * CHUNK)
        def _(i):
            at = me * own + i
            same = jnp.where(chain_cols[...] == chain_ids[at], chain_vec[...], 0.0)
            normed = norm_rows(rows_ref[i].astype(F32) + same).astype(BF16)
            projected = dot(weight[...], normed, NT)
            mask = live_cols * residue_mask[at].astype(F32)
            both = (gate_of(projected[half:]) * projected[:half] * mask).astype(BF16)
            left[:, i] = both[:side].reshape(groups, wide, length)
            right[:, i] = both[side:].reshape(groups, wide, length)

        some = pl.ds(n * CHUNK, CHUNK)
        near = 0
        for d, (p, _, where, same_half) in enumerate(peers):
            leaving.append(send(
                right.at[p, some], right_ref.at[me, some], right_send.at[n, d], right_recv.at[n, d], where
            ))
            if same_half:
                leaving.append(send(
                    left.at[p, some], left_ref.at[mine_in_half, some],
                    left_send.at[n, near], left_recv.at[n, near], where,
                ))
                near += 1
        for k, (a, b) in enumerate((
            (left.at[mine_in_half, some], left_ref.at[mine_in_half, some]),
            (right.at[mine_in_half, some], right_ref.at[me, some]),
        )):
            mine = pltpu.make_async_copy(a, b, out_own.at[n, k])
            mine.start()
            leaving.append(mine)
    for now, _ in arriving:
        for copy in now:
            copy.wait_send()
    for copy in leaving:
        copy.wait()


def multiply(count, left_ref, right_ref, out_ref, scratch):
    lanes = left_ref.shape[1] // 128
    left, right, made = scratch[:lanes], scratch[lanes : 2 * lanes], scratch[2 * lanes :]
    step = left_ref.shape[1]
    for source, flat in ((left_ref, left), (right_ref, right)):

        @pl.loop(0, source.shape[0] // step)
        def _(s):
            at = pl.ds(pl.multiple_of(s * step, step), step)
            for t in range(lanes):
                flat[t][at, :] = source[at, t * 128 : (t + 1) * 128].astype(F32)

    def channel(flat, c):
        at = pl.ds(c, flat[0].shape[0] // count, stride=count)
        return jnp.concatenate([part[at, :].astype(BF16) for part in flat], axis=1)

    for c in range(count):
        product = dot(channel(left, c), channel(right, c), NT)
        for t in range(lanes):
            made[t][pl.ds(c, product.shape[0], stride=count), :] = product[:, t * 128 : (t + 1) * 128]

    tall = out_ref.shape[1]

    @pl.loop(0, out_ref.shape[0])
    def _(g):
        at = pl.ds(pl.multiple_of(g * tall, tall), tall)
        for t in range(lanes):
            out_ref[g, :, t * 128 : (t + 1) * 128] = made[t][at, :].astype(BF16)


def finish_kernel(
    sizes, chain_ids, left_ref, right_ref, pair_ref, chain_row, live_row, chain_vec, tri_gate, tri_out, att_bias,
    att_query, att_kv, att_out,
    out_ref, prod_ref, landed, bias_ref, bias_out, chain_cols, gathered, bias_full,
    after_ref, second_ref, query_ref, key_ref, value_ref, made,
    in_send, in_recv, in_own, row_send, row_recv, col_send, col_recv, sub_send, sub_recv, own_sem,
    out_send, out_recv, out_own, *flat,
):
    nr, nc, ns = sizes
    nq = nc * ns
    r, q, device = position(sizes)
    c, u = lax.axis_index("col"), lax.axis_index("sub")
    me = r * nq + q
    mine_in_half = lax.rem(r, nr // 2) * nq + q
    groups, tall, length = landed.shape
    own = pair_ref.shape[0]
    per = tall // own
    chunks = own // CHUNK
    width = HEADS * HEAD_DIM
    cols = length // nq
    near = [peer for peer in peers_of(sizes) if peer[3]]
    others = [lax.rem(q + d, nq) for d in range(1, nq)]
    meet([peer[2] for peer in peers_of(sizes)])
    multiply(per, left_ref, right_ref, prod_ref, flat)
    arriving = []
    for n in range(chunks):
        some = pl.ds(n * CHUNK * per, CHUNK * per)
        now = [
            send(prod_ref.at[p, some], landed.at[mine_in_half, some], in_send.at[n, d], in_recv.at[n, d], where)
            for d, (p, _, where, _) in enumerate(near)
        ]
        mine = pltpu.make_async_copy(
            prod_ref.at[mine_in_half, some], landed.at[mine_in_half, some], in_own.at[n]
        )
        mine.start()
        arriving.append((now, mine))
    chain_cols[...] = columns_of(chain_row[...])
    live_cols = live_row[...].astype(F32)[None, :]
    for n in range(chunks):
        now, mine = arriving[n]
        mine.wait()
        for copy in now:
            copy.wait_recv()

        @pl.loop(n * CHUNK, (n + 1) * CHUNK)
        def _(i):
            at = pl.ds(pl.multiple_of(i * per, per), per)
            product = landed[:, at, :].astype(F32).reshape(groups * per, length)
            same = jnp.where(chain_cols[...] == chain_ids[me * own + i], chain_vec[...], 0.0)
            start = pair_ref[i].astype(F32) + same
            normed = norm_rows(start).astype(BF16)
            gating = gate_of(dot(normed, tri_gate[...]))
            average = jnp.mean(product, axis=0, keepdims=True)
            centred = product - average
            spread = jnp.mean(centred * centred, axis=0, keepdims=True)
            product_normed = (centred * lax.rsqrt(spread + EPSILON)).astype(BF16)
            after = (start + gating * dot(product_normed, tri_out[...], TN)).astype(BF16)
            second = norm_rows(after.astype(F32)).astype(BF16)
            after_ref[i] = after
            second_ref[i] = second
            bias = dot(att_bias[...], second, (((0,), (1,)), ((), ())))
            bias = jnp.where(live_cols > 0.0, bias, MASKED)
            for h in range(HEADS):
                bias_ref[pl.ds(h * own + i, 1), :] = bias[h : h + 1, :]

    bias_out[...] = bias_ref[...].astype(BF16)
    mine = pltpu.make_async_copy(bias_out, gathered.at[q, r], own_sem)
    mine.start()
    hops = []
    for d in range(1, nr):
        hops.append(send(
            bias_out, gathered.at[q, r], row_send.at[d - 1], row_recv.at[d - 1],
            device(lax.rem(r + d, nr), q),
        ))

    def prepare(first, past):
        @pl.loop(first, past)
        def _(i):
            second = second_ref[i]
            query = dot(second, att_query[:, :width])
            query_ref[i] = (query * HEAD_DIM ** (-0.5)).astype(BF16)
            keyval = dot(second, att_kv[...]).astype(BF16)
            key_ref[i] = keyval[:, :width]
            value_ref[i] = keyval[:, width:]

    prepare(0, own // 2)
    mine.wait()
    for copy in hops:
        copy.wait_recv()
    across = []
    for d in range(1, nc):
        across.append(send(
            gathered.at[q], gathered.at[q], col_send.at[d - 1], col_recv.at[d - 1],
            device(r, lax.rem(c + d, nc) * ns + u),
        ))
    last = []

    def pass_on(e):
        source = lax.rem(c + nc - e, nc) * ns + u
        for d in range(1, ns):
            last.append(send(
                gathered.at[source], gathered.at[source], sub_send.at[e, d - 1], sub_recv.at[e, d - 1],
                device(r, c * ns + lax.rem(u + d, ns)),
            ))

    pass_on(0)
    prepare(own // 2, own)
    for e, copy in enumerate(across):
        copy.wait_recv()
        pass_on(e + 1)
    for copy in last:
        copy.wait()
    for copy in hops + across:
        copy.wait_send()
    for now, _ in arriving:
        for copy in now:
            copy.wait_send()
    for row in range(nr):
        for place in range(nq):
            block = gathered[place, row].astype(F32)
            for h in range(HEADS):
                bias_full[h, (row * nq + place) * own : (row * nq + place + 1) * own, :] = block[h * own : (h + 1) * own]
    head = lax.broadcasted_iota(jnp.int32, (length, width), 1) // HEAD_DIM
    leaving = []
    for n in range(own // CHUNK):

        @pl.loop(n * CHUNK, (n + 1) * CHUNK)
        def _(i):
            second = second_ref[i]
            gating = gate_of(dot(second, att_query[:, width:]))
            query, key, value = query_ref[i], key_ref[i], value_ref[i]
            summed = None
            for h in range(HEADS):
                mine = (head == h).astype(BF16)
                scores = dot(query * mine, key, NT) + bias_full[h]
                weights = jnp.exp(scores).astype(BF16)
                part = dot(weights, jnp.concatenate([value * mine, mine], axis=1))
                summed = part if summed is None else summed + part
            attended = summed[:, :width] / summed[:, width:]
            outgoing = (attended * gating).astype(BF16)
            result = after_ref[i].astype(F32) + dot(outgoing, att_out[...])
            made[i] = result.astype(BF16)

        some = pl.ds(n * CHUNK, CHUNK)
        to = pl.ds(q * own + n * CHUNK, CHUNK)
        for d, p in enumerate(others):
            leaving.append(send(
                made.at[some, pl.ds(p * cols, cols), :], out_ref.at[to],
                out_send.at[n, d], out_recv.at[n, d], device(r, p),
            ))
        mine = pltpu.make_async_copy(made.at[some, pl.ds(q * cols, cols), :], out_ref.at[to], out_own.at[n])
        mine.start()
        leaving.append(mine)
    for copy in leaving:
        copy.wait()


def by_rows(
    sizes,
    pair,
    chain_ids,
    residue_mask,
    chain_vec,
    tri_in,
    tri_gate,
    tri_out,
    att_query,
    att_kv,
    att_bias,
    att_out,
):
    nr, nc, ns = sizes
    nq = nc * ns
    groups = nr * nq
    rows, cols, channels = pair.shape
    own = rows // nq
    length = cols * nq
    near = groups // 2
    per = channels // near
    chain_row, live_row, chain_one = chain_ids, residue_mask, chain_vec[None, :]
    order = [tri_in[:, n * channels : (n + 1) * channels] for n in (0, 2, 1, 3)]
    weight = jnp.concatenate(order, axis=1).T

    chunks = own // CHUNK
    smem = pl.BlockSpec(memory_space=pltpu.SMEM)
    vmem = pl.BlockSpec(memory_space=pltpu.VMEM)
    anywhere = pl.BlockSpec(memory_space=pl.ANY)
    dma = pltpu.SemaphoreType.DMA
    row_shape = jax.ShapeDtypeStruct((own, length, channels), BF16)

    def params(n):
        return pltpu.CompilerParams(collective_id=n, has_side_effects=True, vmem_limit_bytes=VMEM_LIMIT)

    side_shape = (near, own, per, length)
    pair_rows, left, right = pl.pallas_call(
        functools.partial(project_kernel, sizes),
        in_specs=[smem, smem, vmem, vmem, vmem, vmem, anywhere],
        out_specs=[vmem, anywhere, anywhere],
        out_shape=[
            row_shape,
            jax.ShapeDtypeStruct(side_shape, BF16),
            jax.ShapeDtypeStruct((groups, own, per, length), BF16),
        ],
        scratch_shapes=[
            pltpu.VMEM(side_shape, BF16), pltpu.VMEM(side_shape, BF16), pltpu.VMEM((length, channels), jnp.int32),
            dma((chunks, nq - 1)), dma((chunks, nq - 1)), dma((chunks,)),
            dma((chunks, near - 1)), dma((chunks, near - 1)),
            dma((chunks, groups - 1)), dma((chunks, groups - 1)), dma((chunks, 2)),
        ],
        compiler_params=params(1),
        name="project",
    )(chain_ids, residue_mask, chain_row, live_row, chain_one, weight, pair)
    lanes = length // 128
    tall_left, tall_right = near * own * per, length * per
    tall = HEADS * own
    rows_bf16 = pltpu.VMEM(row_shape.shape, BF16)
    return pl.pallas_call(
        functools.partial(finish_kernel, sizes),
        in_specs=[smem] + [vmem] * 12,
        out_specs=anywhere,
        out_shape=jax.ShapeDtypeStruct((rows, cols, channels), BF16),
        scratch_shapes=[
            pltpu.VMEM((near, own * per, length), BF16), pltpu.VMEM((near, own * per, length), BF16),
            pltpu.VMEM((tall, length), F32), pltpu.VMEM((tall, length), BF16),
            pltpu.VMEM((length, channels), jnp.int32),
            pltpu.VMEM((nq, nr, tall, length), BF16), pltpu.VMEM((HEADS, length, length), F32),
            rows_bf16, rows_bf16, rows_bf16, rows_bf16, rows_bf16, rows_bf16,
            dma((chunks, near - 1)), dma((chunks, near - 1)), dma((chunks,)),
            dma((max(nr - 1, 1),)), dma((max(nr - 1, 1),)),
            dma((max(nc - 1, 1),)), dma((max(nc - 1, 1),)),
            dma((nc, max(ns - 1, 1))), dma((nc, max(ns - 1, 1))), dma,
            dma((chunks, nq - 1)), dma((chunks, nq - 1)), dma((chunks,)),
        ]
        + [pltpu.VMEM((tall_left, 128), F32)] * lanes
        + [pltpu.VMEM((tall_right, 128), F32)] * lanes
        + [pltpu.VMEM((tall_left, 128), F32)] * lanes,
        compiler_params=params(2),
        name="finish",
    )(
        chain_ids, left.reshape(tall_left, length), right.reshape(tall_right, length), pair_rows,
        chain_row, live_row, chain_one, tri_gate, tri_out, att_bias, att_query, att_kv, att_out,
    )


def device_program(sizes, pair, *rest):
    rows, cols, channels = pair.shape
    nr, nc, ns = sizes
    nq = nc * ns
    length = cols * nq
    fits = (
        rows % (2 * nq) == 0
        and (rows // nq) % 8 == 0
        and cols % 16 == 0
        and channels == 128
        and nr % 2 == 0
        and channels == 8 * nr * nq
        and length % 128 == 0
        and length == rows * nr
    )
    if fits:
        return by_rows(sizes, pair, *rest)
    return on_device(pair, *rest)


def solution(mesh):
    sizes = tuple(mesh.shape[name] for name in ("row", "col", "sub"))
    return jax.shard_map(
        functools.partial(device_program, sizes),
        mesh=mesh,
        in_specs=(
            P(("grp", "row"), ("col", "sub"), None),
            P("grp"),
            P("grp"),
            P(),
            P(),
            P(),
            P(),
            P(),
            P(),
            P(),
            P(),
        ),
        out_specs=P(("grp", "row"), ("col", "sub"), None),
        check_vma=False,
    )
```
